32 devices in a mesh: parts: 2 (over y), cand: 4 (over z), query: 4 (over x, core).
Axes of the slice: x: 2, y: 2, z: 4, core: 2. Of those that a mesh axis runs over, the one named last changes fastest.
Arguments:
- cand_out: bfloat16 [24, 4, 5120], P(('parts', 'cand')), parts along dimension 0, may hold values from -6 to 6
- cand_in: bfloat16 [24, 4, 13824], P(('parts', 'cand')), parts along dimension 0, may hold values from -6 to 6
- query_out: bfloat16 [32, 8, 5120], P(('parts', 'query')), parts along dimension 0, may hold values from -0.03125 to 0.03125
- query_in: bfloat16 [32, 8, 13824], P(('parts', 'query')), parts along dimension 0, may hold values from -0.02734375 to 0.02734375
- eigenvalues: bfloat16 [4, 2560, 6912], P('cand'), may hold values from 0.19921875 to 5
- slot_blocks: int32 [8, 4, 2], P(('parts', 'query')), parts along dimension 0, may hold values from 0 to 2, as said below
- live_counts: int32 [8, 4], P(('parts', 'query')), parts along dimension 0, may hold values from 1 to 2, as said below
Outputs:
- scores: float32 [32, 4, 2], P(('parts', 'query'), 'cand'), parts along dimension 0
The draws below stay inside these ranges and needn't reach their ends.
There are 2 independent parts, one for each index of `parts`. The reference program is written for one: setup_inputs(seed, part) draws one part's arguments, and reference() takes and returns one part's arrays. A program takes and returns all parts, laid end to end along the dimension named above; an argument that names none is the same for every part. Nothing has to cross between parts.
Inputs may be any that keep to these rules, and one draw needn't show every extreme that they name: slot_blocks[g, k] holds 2 distinct blocks of the 3 blocks of source k. `live_counts`: every group has a source whose 2 slots are all used.
All inputs are finite; a program needn't handle non-finite values.
Results may differ from the reference program's by a relative error of at most 0.0029.
Values may be sent and summed in bfloat16 or wider, within the bound.
No kernel may reach another device: no remote copies, remote signals or barrier semaphores. Data moves between devices by JAX's collectives and lax.ppermute only.
A program may use at most 192 MiB of HBM per device.

```python
import math
import jax
import jax.numpy as jnp
from jax import lax

DO = 5120
DI = 13824
R = 8
QG = 4
BLK_DEV = 3
BT = 4
CAP = 2
NQ = 16
NB = 12
TILES = 4
TC = 2
TROWS = 2560
TCOLS = 6912
N_CAND = 4
N_QUERY = 4


def draw_slot_blocks(key, part):
    subkeys = jax.random.split(key, N_QUERY * N_CAND)

    def single(subkey):
        return jax.random.permutation(subkey, BLK_DEV)[:CAP]
    return jax.vmap(single)(subkeys).reshape(N_QUERY, N_CAND, CAP).astype(jnp.int32)


def draw_live_counts(key, part):
    drawing = jax.random.fold_in(key, 11)
    forcing = jax.random.fold_in(key, 23)
    drawn = jax.random.randint(drawing, (N_QUERY, N_CAND), 1, CAP + 1)
    fullest = jax.random.randint(forcing, (N_QUERY, 1), 0, N_CAND)
    column = jnp.arange(N_CAND, dtype=jnp.int32)[None, :]
    return jnp.where(column == fullest, CAP, drawn).astype(jnp.int32)


def levels(stream_key, dims, cuts, least, top_value):
    def one(axis_at, parts):
        heights = jax.random.uniform(jax.random.fold_in(jax.random.fold_in(stream_key, 6), axis_at), (parts,), jnp.float32, least / len(cuts), top_value / len(cuts))
        return jnp.repeat(jnp.exp(heights), dims[axis_at] // parts).reshape((-1,) + (1,) * (len(dims) - axis_at - 1))

    level = one(*cuts[0])
    for cut in cuts[1:]:
        level = level * one(*cut)
    return level


def scatter_about(stream_key, dims, deviation, bound, shards=(), kind=jnp.bfloat16):
    values = deviation * jax.random.normal(stream_key, dims, jnp.float32)
    if shards:
        values = values * levels(stream_key, dims, shards, -0.22, 0.18)
    return jnp.clip(values, -bound, bound).astype(kind)


def setup_inputs(seed: int = 0, part: int = 0) -> dict:
    keys = jax.random.split(jax.random.key(seed), 8)
    part_splits = jax.random.split(jax.random.fold_in(keys[7], part), 8)
    return {
        "cand_out": scatter_about(part_splits[0], (NB, BT, DO), 1.0, 6.0, ((0, 4),)),
        "cand_in": scatter_about(part_splits[1], (NB, BT, DI), 1.0, 6.0, ((0, 4),)),
        "query_out": scatter_about(part_splits[2], (NQ, R, DO), (DO * R) ** -0.5, 0.03125, ((0, 4),)),
        "query_in": scatter_about(part_splits[3], (NQ, R, DI), (DI * BT) ** -0.5, 0.02734375, ((0, 4),)),
        "eigenvalues": jnp.clip(jnp.exp(math.log(5.0) - 3.2227897 * jax.random.uniform(keys[4], (TILES, TROWS, TCOLS), jnp.float32) ** levels(keys[4], (TILES, TROWS, TCOLS), ((0, 4),), -0.2, 0.2)), 0.19921875, 5.0).astype(jnp.bfloat16),
        "slot_blocks": draw_slot_blocks(jax.random.fold_in(jax.random.fold_in(keys[7], part), 71), part),
        "live_counts": draw_live_counts(jax.random.fold_in(jax.random.fold_in(keys[7], part), 71), part),
    }


DAMPING = 0.05


def reference(cand_out, cand_in, query_out, query_in, eigenvalues, slot_blocks, live_counts):
    block_index = jnp.arange(N_CAND, dtype=jnp.int32)[None, :, None] * BLK_DEV + slot_blocks
    live_slots = (jnp.arange(CAP, dtype=jnp.int32)[None, None, :] < live_counts[:, :, None]).astype(jnp.float32)
    group_index = jnp.arange(NQ, dtype=jnp.int32) // QG
    query_blocks = block_index[group_index].reshape(NQ, N_CAND * CAP)
    query_live = live_slots[group_index]

    def add_tile(running, tile_index):
        row_part = tile_index // TC
        col_part = tile_index % TC
        out_factor = lax.dynamic_slice_in_dim(query_out, row_part * TROWS, TROWS, 2).astype(jnp.float32)
        in_factor = lax.dynamic_slice_in_dim(query_in, col_part * TCOLS, TCOLS, 2).astype(jnp.float32)
        outer_sum = jnp.einsum('qri,qrj->qij', out_factor, in_factor, precision=lax.Precision.HIGHEST)
        precond = (outer_sum / (eigenvalues[tile_index].astype(jnp.float32) + DAMPING)).astype(jnp.bfloat16)
        out_tile = lax.dynamic_slice_in_dim(cand_out, row_part * TROWS, TROWS, 2).astype(jnp.float32)
        in_tile = lax.dynamic_slice_in_dim(cand_in, col_part * TCOLS, TCOLS, 2).astype(jnp.float32)
        block_grads = jnp.einsum('bti,btj->bij', out_tile, in_tile, precision=lax.Precision.HIGHEST)
        all_scores = jnp.einsum('qij,bij->qb', precond.astype(jnp.float32), block_grads, precision=lax.Precision.HIGHEST)
        picked = jnp.take_along_axis(all_scores, query_blocks, axis=1).reshape(NQ, N_CAND, CAP)
        return running + picked * query_live, None

    start = jnp.zeros((NQ, N_CAND, CAP), jnp.float32)
    result, _ = lax.scan(add_tile, start, jnp.arange(N_CAND, dtype=jnp.int32))
    return result
```

```python
import functools

import jax
import jax.numpy as jnp
from jax import lax
from jax.experimental import pallas as pl
from jax.experimental.pallas import tpu as pltpu
from jax.sharding import PartitionSpec as P

DAMPING = 0.05


def score_kernel(lam_ref, left_ref, right_ref, out_ref, acc_ref, *, width):
    @pl.when(pl.program_id(0) == 0)
    def _():
        acc_ref[...] = jnp.zeros_like(acc_ref)

    queries = left_ref.shape[0]

    @pl.loop(0, lam_ref.shape[1] // width)
    def _(chunk):
        if width == lam_ref.shape[1]:
            cols = slice(None)
        else:
            cols = pl.ds(pl.multiple_of(chunk * width, 128), width)
        inverse = 1.0 / (lam_ref[:, cols].astype(jnp.float32) + DAMPING)
        for q in range(queries):
            outer = jnp.dot(left_ref[q], right_ref[q, :, cols], preferred_element_type=jnp.float32)
            precond = (outer * inverse).astype(jnp.bfloat16)
            acc_ref[q, :, cols] += jnp.dot(
                out_ref[...], precond, preferred_element_type=jnp.float32
            )


def pick(total, unit, limit):
    best = total
    if total % unit == 0:
        for size in range(unit, min(total, limit) + 1, unit):
            if total % size == 0:
                best = size
    return best


def mapped_tokens(lam, left, right, out_tokens):
    rows, cols = lam.shape
    queries, depth = right.shape[:2]
    tokens = out_tokens.shape[0]
    height = pick(rows, 128, 256)
    width = pick(cols, 128, 2304)
    return pl.pallas_call(
        functools.partial(score_kernel, width=width),
        grid=(rows // height,),
        in_specs=[
            pl.BlockSpec((height, cols), lambda i: (i, 0)),
            pl.BlockSpec((queries, height, depth), lambda i: (0, i, 0)),
            pl.BlockSpec((queries, depth, cols), lambda i: (0, 0, 0)),
            pl.BlockSpec((tokens, height), lambda i: (0, i)),
        ],
        out_specs=pl.BlockSpec((queries, tokens, cols), lambda i: (0, 0, 0)),
        out_shape=jax.ShapeDtypeStruct((queries, tokens, cols), jnp.float32),
        compiler_params=pltpu.CompilerParams(vmem_limit_bytes=60 << 20),
        cost_estimate=pl.CostEstimate(
            flops=2 * queries * rows * cols * (depth + tokens),
            bytes_accessed=2 * rows * cols,
            transcendentals=rows * cols,
        ),
    )(lam, left, right, out_tokens)


def body(cand_out, cand_in, query_out, query_in, eigenvalues, slot_blocks, live_counts):
    tile_count = lax.axis_size("cand")
    row_tiles = min(8, max(2, tile_count // 8))
    col_tiles = tile_count // row_tiles
    position = lax.axis_index("cand")
    row_part = position // col_tiles
    col_part = position % col_tiles
    tokens = cand_out.shape[1]
    row_width = cand_out.shape[2] // row_tiles
    col_width = cand_in.shape[2] // col_tiles
    slot_count = slot_blocks.shape[2]
    queries = query_out.shape[0]

    own_slots = lax.dynamic_index_in_dim(slot_blocks[0], position, 0, keepdims=False)
    chosen_out = jnp.take(cand_out, own_slots, axis=0, mode="clip")
    chosen_in = jnp.take(cand_in, own_slots, axis=0, mode="clip")
    per_source = slot_count * tokens
    out_parts = jnp.moveaxis(chosen_out.reshape(per_source, row_tiles, row_width), 1, 0)
    out_parts = jnp.broadcast_to(
        out_parts[:, None], (row_tiles, col_tiles, per_source, row_width)
    ).reshape(tile_count, per_source, row_width)
    in_parts = jnp.moveaxis(chosen_in.reshape(per_source, col_tiles, col_width), 1, 0)
    in_parts = jnp.broadcast_to(
        in_parts[None], (row_tiles, col_tiles, per_source, col_width)
    ).reshape(tile_count, per_source, col_width)
    out_tokens = lax.all_to_all(out_parts, "cand", split_axis=0, concat_axis=0, tiled=True)
    in_tokens = lax.all_to_all(in_parts, "cand", split_axis=0, concat_axis=0, tiled=True)
    out_tokens = out_tokens.reshape(tile_count * per_source, row_width)
    in_tokens = in_tokens.reshape(tile_count * per_source, col_width)

    out_factor = lax.dynamic_slice_in_dim(query_out, row_part * row_width, row_width, 2)
    in_factor = lax.dynamic_slice_in_dim(query_in, col_part * col_width, col_width, 2)
    left = jnp.swapaxes(out_factor, 1, 2)

    mapped = mapped_tokens(eigenvalues[0], left, in_factor, out_tokens)
    totals = jnp.sum(mapped * in_tokens.astype(jnp.float32)[None], axis=2)
    totals = totals.reshape(queries, tile_count, slot_count, tokens).sum(axis=3)
    gathered = lax.all_to_all(
        jnp.moveaxis(totals, 1, 0), "cand", split_axis=0, concat_axis=0, tiled=True
    )
    scores = jnp.sum(gathered, axis=0)
    own_live = lax.dynamic_index_in_dim(live_counts[0], position, 0, keepdims=False)
    used = jnp.arange(slot_count, dtype=jnp.int32) < own_live
    return jnp.where(used[None], scores, 0.0)[:, None, :]


def solution(mesh):
    return jax.shard_map(
        body,
        mesh=mesh,
        in_specs=(
            P(("parts", "cand"), None, None),
            P(("parts", "cand"), None, None),
            P(("parts", "query"), None, None),
            P(("parts", "query"), None, None),
            P("cand", None, None),
            P(("parts", "query"), None, None),
            P(("parts", "query"), None),
        ),
        out_specs=P(("parts", "query"), "cand", None),
        check_vma=False,
    )
```

```python
import functools

import jax
import jax.numpy as jnp
from jax import lax
from jax.experimental import pallas as pl
from jax.experimental.pallas import tpu as pltpu
from jax.sharding import PartitionSpec as P

DAMPING = 0.05
PIECE = 512
BEHIND = 2
MAX_SHIFTS = 8


def pack_kernel(place_ref, *refs, slots, shifts, row_tiles, col_tiles, by_shift):
    outs, ins = refs[:slots], refs[slots : 2 * slots]
    results = refs[2 * slots :]
    position = place_ref[slots]
    tokens = outs[0].shape[1]
    row_width = outs[0].shape[2] // row_tiles
    col_width = ins[0].shape[2] // col_tiles

    def store(sources, target, part, width, parts):
        for piece in range(parts):

            @pl.when(part == piece)
            def _():
                for slot, source in enumerate(sources):
                    target[slot * tokens : (slot + 1) * tokens, :] = source[
                        0, :, piece * width : (piece + 1) * width
                    ]

    for shift in range(shifts):
        if by_shift:
            tile = lax.rem(position + shift, shifts)
            targets = results[shift], results[shifts + shift]
        else:
            tile = jnp.int32(shift)
            targets = results[0].at[shift], results[1].at[shift]
        store(outs, targets[0], tile // col_tiles, row_width, row_tiles)
        store(ins, targets[1], lax.rem(tile, col_tiles), col_width, col_tiles)


def pack_tokens(cand_out, cand_in, own_slots, position, row_tiles, col_tiles, shifts, by_shift):
    slots = own_slots.shape[0]
    tokens = cand_out.shape[1]
    rows = slots * tokens
    widths = cand_out.shape[2] // row_tiles, cand_in.shape[2] // col_tiles
    place = jnp.concatenate([own_slots, position[None].astype(jnp.int32)])

    def listed(slot):
        return lambda i, place_ref: (place_ref[slot], 0, 0)

    specs = [
        pl.BlockSpec((1, tokens, array.shape[2]), listed(slot))
        for array in (cand_out, cand_in)
        for slot in range(slots)
    ]
    if by_shift:
        shapes = [(rows, width) for width in widths for _ in range(shifts)]
    else:
        shapes = [(shifts, rows, width) for width in widths]
    return pl.pallas_call(
        functools.partial(
            pack_kernel,
            slots=slots,
            shifts=shifts,
            row_tiles=row_tiles,
            col_tiles=col_tiles,
            by_shift=by_shift,
        ),
        grid_spec=pltpu.PrefetchScalarGridSpec(
            num_scalar_prefetch=1,
            grid=(1,),
            in_specs=specs,
            out_specs=[
                pl.BlockSpec(shape, lambda i, place_ref, n=len(shape): (0,) * n)
                for shape in shapes
            ],
        ),
        out_shape=[jax.ShapeDtypeStruct(shape, cand_out.dtype) for shape in shapes],
    )(place, *([cand_out] * slots), *([cand_in] * slots))


def map_kernel(part_ref, lam_ref, left_ref, right_ref, *refs):
    del part_ref
    out_refs, acc_ref, out_buf = refs[:-2], refs[-2], refs[-1]

    @pl.when(pl.program_id(0) == 0)
    def _():
        acc_ref[...] = jnp.zeros_like(acc_ref)

    start = 0
    for ref in out_refs:
        out_buf[start : start + ref.shape[0], :] = ref[...]
        start += ref.shape[0]
    queries = left_ref.shape[0]
    cols = lam_ref.shape[2]
    lefts = [left_ref[q].astype(jnp.float32).T.astype(jnp.bfloat16) for q in range(queries)]
    waiting = []

    def contract():
        q, begin, end, precond = waiting.pop(0)
        acc_ref[q, :, begin:end] += jnp.dot(
            out_buf[...], precond, preferred_element_type=jnp.float32
        )

    for begin in range(0, cols, PIECE):
        end = min(begin + PIECE, cols)
        inverse = 1.0 / (lam_ref[0, :, begin:end].astype(jnp.float32) + DAMPING)
        for q in range(queries):
            outer = jnp.dot(
                lefts[q], right_ref[q, :, begin:end], preferred_element_type=jnp.float32
            )
            if len(waiting) >= BEHIND:
                contract()
            waiting.append((q, begin, end, (outer * inverse).astype(jnp.bfloat16)))
    while waiting:
        contract()


def pick(total, unit, limit):
    best = total
    if total % unit == 0:
        for size in range(unit, min(total, limit) + 1, unit):
            if total % size == 0:
                best = size
    return best


def map_tokens(lam, query_out, query_in, row_part, col_part, out_tokens):
    rows, cols = lam.shape[1:]
    queries, depth = query_in.shape[:2]
    tokens = sum(part.shape[0] for part in out_tokens)
    height = pick(rows, 128, 256)
    steps = rows // height
    if cols % 128:
        query_in = lax.dynamic_slice_in_dim(query_in, col_part * cols, cols, 2)
        col_part = jnp.zeros_like(col_part)
    parts = jnp.stack([row_part, col_part]).astype(jnp.int32)
    grant = (16 << 20) + 8 * queries * tokens * cols + 4 * height * cols
    return pl.pallas_call(
        map_kernel,
        grid_spec=pltpu.PrefetchScalarGridSpec(
            num_scalar_prefetch=1,
            grid=(steps,),
            in_specs=[
                pl.BlockSpec((1, height, cols), lambda i, part: (0, i, 0)),
                pl.BlockSpec((queries, depth, height), lambda i, part: (0, 0, part[0] * steps + i)),
                pl.BlockSpec((queries, depth, cols), lambda i, part: (0, 0, part[1])),
            ]
            + [pl.BlockSpec((part.shape[0], height), lambda i, part: (0, i)) for part in out_tokens],
            out_specs=pl.BlockSpec((queries, tokens, cols), lambda i, part: (0, 0, 0)),
            scratch_shapes=[pltpu.VMEM((tokens, height), jnp.bfloat16)],
        ),
        out_shape=jax.ShapeDtypeStruct((queries, tokens, cols), jnp.float32),
        compiler_params=pltpu.CompilerParams(vmem_limit_bytes=grant),
        cost_estimate=pl.CostEstimate(
            flops=2 * queries * rows * cols * (depth + tokens),
            bytes_accessed=2 * rows * cols,
            transcendentals=rows * cols,
        ),
    )(parts, lam, query_out, query_in, *out_tokens)


def fold_kernel(mapped_ref, *refs):
    half = len(refs) // 2
    start = 0
    for in_ref, score_ref in zip(refs[:half], refs[half:]):
        stop = start + in_ref.shape[0]
        product = mapped_ref[:, start:stop, :] * in_ref[...].astype(jnp.float32)[None]
        part = jnp.sum(product, axis=2)
        start = stop

        @pl.when(pl.program_id(0) == 0)
        def _():
            score_ref[...] = part

        @pl.when(pl.program_id(0) > 0)
        def _():
            score_ref[...] += part


def fold_tokens(mapped, in_tokens):
    queries, tokens, cols = mapped.shape
    width = pick(cols, 128, 1536)
    grant = min((4 << 20) + 24 * queries * tokens * width, 56 << 20)
    return pl.pallas_call(
        fold_kernel,
        grid=(cols // width,),
        in_specs=[pl.BlockSpec((queries, tokens, width), lambda i: (0, 0, i))]
        + [pl.BlockSpec((part.shape[0], width), lambda i: (0, i)) for part in in_tokens],
        out_specs=[pl.BlockSpec((queries, part.shape[0]), lambda i: (0, 0)) for part in in_tokens],
        out_shape=[
            jax.ShapeDtypeStruct((queries, part.shape[0]), jnp.float32) for part in in_tokens
        ],
        compiler_params=pltpu.CompilerParams(vmem_limit_bytes=grant),
    )(mapped, *in_tokens)


def exchange(array):
    return lax.all_to_all(array, "cand", split_axis=0, concat_axis=0, tiled=True)


def shifted(array, shift, devices):
    pairs = [(device, (device + shift) % devices) for device in range(devices)]
    return lax.ppermute(array, "cand", pairs)


def body(cand_out, cand_in, query_out, query_in, eigenvalues, slot_blocks, live_counts):
    tile_count = lax.axis_size("cand")
    row_tiles = min(8, max(2, tile_count // 8))
    col_tiles = tile_count // row_tiles
    position = lax.axis_index("cand")
    row_part = position // col_tiles
    col_part = position % col_tiles
    tokens = cand_out.shape[1]
    slot_count = slot_blocks.shape[2]
    queries = query_out.shape[0]
    by_shift = tile_count <= MAX_SHIFTS

    own_slots = lax.dynamic_index_in_dim(slot_blocks[0], position, 0, keepdims=False)
    packed = pack_tokens(
        cand_out, cand_in, own_slots, position, row_tiles, col_tiles, tile_count, by_shift
    )
    if by_shift:
        out_tokens = [packed[0]] + [
            shifted(packed[shift], shift, tile_count) for shift in range(1, tile_count)
        ]
        in_tokens = [packed[tile_count]] + [
            shifted(packed[tile_count + shift], shift, tile_count)
            for shift in range(1, tile_count)
        ]
    else:
        out_tokens = [exchange(packed[0]).reshape(-1, packed[0].shape[2])]
        in_tokens = [exchange(packed[1]).reshape(-1, packed[1].shape[2])]

    mapped = map_tokens(eigenvalues, query_out, query_in, row_part, col_part, out_tokens)
    folded = fold_tokens(mapped, in_tokens)
    if by_shift:
        total = folded[0]
        for shift in range(1, tile_count):
            total = total + shifted(folded[shift], -shift, tile_count)
    else:
        parts = jnp.moveaxis(folded[0].reshape(queries, tile_count, -1), 1, 0)
        total = jnp.sum(exchange(parts), axis=0)
    scores = total.reshape(queries, slot_count, tokens).sum(axis=2)
    own_live = lax.dynamic_index_in_dim(live_counts[0], position, 0, keepdims=False)
    used = jnp.arange(slot_count, dtype=jnp.int32) < own_live
    return jnp.where(used[None], scores, 0.0)[:, None, :]


def solution(mesh):
    return jax.shard_map(
        body,
        mesh=mesh,
        in_specs=(
            P(("parts", "cand"), None, None),
            P(("parts", "cand"), None, None),
            P(("parts", "query"), None, None),
            P(("parts", "query"), None, None),
            P("cand", None, None),
            P(("parts", "query"), None, None),
            P(("parts", "query"), None),
        ),
        out_specs=P(("parts", "query"), "cand", None),
        check_vma=False,
    )
```

```python
import functools

import jax
import jax.numpy as jnp
from jax import lax
from jax.experimental import pallas as pl
from jax.experimental.pallas import tpu as pltpu
from jax.sharding import PartitionSpec as P

DAMPING = 0.05
PIECE = 512
BEHIND = 2
MAX_SHIFTS = 8
GRANT_AHEAD = 62 << 20
GRANT_MAIN = 48 << 20
GRANT_AHEAD = 48 << 20
GRANT_MAIN = 48 << 20


def pack_kernel(list_ref, out_ref, in_ref, *results, row_tiles, col_tiles, shifts, by_shift):
    position = lax.axis_index("cand")
    slots = list_ref.shape[1]
    tokens = out_ref.shape[1]
    row_width = out_ref.shape[2] // row_tiles
    col_width = in_ref.shape[2] // col_tiles

    def store(source, target, first, part, width, parts):
        for piece in range(parts):

            @pl.when(part == piece)
            def _():
                for slot in range(slots):
                    block = list_ref[0, slot, position]
                    target[slot * tokens : (slot + 1) * tokens, first : first + width] = source[
                        block, :, piece * width : (piece + 1) * width
                    ]

    for shift in range(shifts):
        if by_shift:
            tile = lax.rem(position + shift, shifts)
            target = results[shift]
        else:
            tile = jnp.int32(shift)
            target = results[0].at[shift]
        store(out_ref, target, 0, tile // col_tiles, row_width, row_tiles)
        store(in_ref, target, row_width, lax.rem(tile, col_tiles), col_width, col_tiles)


def whole(array):
    return pl.BlockSpec(array.shape, lambda *i: (0,) * len(array.shape))


def pack_tokens(cand_out, cand_in, slot_blocks, row_tiles, col_tiles, shifts, by_shift):
    lists = jnp.swapaxes(slot_blocks, 1, 2)
    rows = slot_blocks.shape[2] * cand_out.shape[1]
    width = cand_out.shape[2] // row_tiles + cand_in.shape[2] // col_tiles
    if by_shift:
        shapes = [(rows, width)] * shifts
    else:
        shapes = [(shifts, rows, width)]
    results = [jax.ShapeDtypeStruct(shape, cand_out.dtype) for shape in shapes]
    return pl.pallas_call(
        functools.partial(
            pack_kernel,
            row_tiles=row_tiles,
            col_tiles=col_tiles,
            shifts=shifts,
            by_shift=by_shift,
        ),
        grid=(1,),
        in_specs=[pl.BlockSpec(memory_space=pltpu.SMEM), whole(cand_out), whole(cand_in)],
        out_specs=[whole(result) for result in results],
        out_shape=results,
    )(lists, cand_out, cand_in)


class Factors:
    def __init__(self, left_ref, right_ref, height, cols, row_tiles, col_tiles):
        position = lax.axis_index("cand")
        self.left_ref, self.right_ref = left_ref, right_ref
        self.height, self.cols = height, cols
        self.row_start = (position // col_tiles) * (left_ref.shape[2] // row_tiles)
        self.split = right_ref.shape[2] != cols
        self.col_start = lax.rem(position, col_tiles) * cols

    def left(self, query, block):
        start = pl.multiple_of(self.row_start + block * self.height, 128)
        rows = self.left_ref[query, :, pl.ds(start, self.height)]
        return rows.astype(jnp.float32).T.astype(jnp.bfloat16)

    def right(self, query, begin, end):
        if not self.split:
            return self.right_ref[query, :, begin:end]
        start = pl.multiple_of(self.col_start + begin, 128)
        return self.right_ref[query, :, pl.ds(start, end - begin)]


def spans(cols):
    return [(begin, min(begin + PIECE, cols)) for begin in range(0, cols, PIECE)]


def damped_inverse(lam_ref, begin, end):
    return 1.0 / (lam_ref[0, :, begin:end].astype(jnp.float32) + DAMPING)


def ahead_kernel(lam_ref, left_ref, right_ref, stored_ref, *, row_tiles, col_tiles):
    queries, height, cols = stored_ref.shape
    factors = Factors(left_ref, right_ref, height, cols, row_tiles, col_tiles)
    lefts = [factors.left(q, pl.program_id(0)) for q in range(queries)]
    for begin, end in spans(cols):
        inverse = damped_inverse(lam_ref, begin, end)
        for q in range(queries):
            outer = jnp.dot(
                lefts[q], factors.right(q, begin, end), preferred_element_type=jnp.float32
            )
            stored_ref[q, :, begin:end] = (outer * inverse).astype(jnp.bfloat16)


def score_kernel(lam_ref, left_ref, right_ref, *refs, ahead, tokens, results, row_tiles, col_tiles):
    token_refs, refs = refs[:results], refs[results:]
    stored_ref = None
    if ahead:
        stored_ref, refs = refs[0], refs[1:]
    score_refs, (acc_ref, token_buf) = refs[:results], refs[results:]
    queries, height, cols = left_ref.shape[0], lam_ref.shape[1], lam_ref.shape[2]
    step = pl.program_id(0)
    row_width = token_buf.shape[1]

    @pl.when(step == 0)
    def _():
        acc_ref[...] = jnp.zeros_like(acc_ref)
        start = 0
        for ref in token_refs:
            token_buf[start : start + ref.shape[0], :] = ref[:, :row_width]
            start += ref.shape[0]

    def token_rows(block):
        return token_buf[:, pl.ds(pl.multiple_of(block * height, 128), height)]

    factors = Factors(left_ref, right_ref, height, cols, row_tiles, col_tiles)
    lefts = [factors.left(q, step + ahead) for q in range(queries)]
    rows = token_rows(step + ahead)
    extra = []
    if ahead:
        for item in range(stored_ref.shape[0]):
            index = step * stored_ref.shape[0] + item
            extra.append((item, lax.rem(index, queries), token_rows(index // queries)))
    waiting = []

    def contract():
        q, begin, end, precond = waiting.pop(0)
        acc_ref[q, :, begin:end] += jnp.dot(rows, precond, preferred_element_type=jnp.float32)

    for begin, end in spans(cols):
        inverse = damped_inverse(lam_ref, begin, end)
        for q in range(queries):
            outer = jnp.dot(
                lefts[q], factors.right(q, begin, end), preferred_element_type=jnp.float32
            )
            if len(waiting) >= BEHIND:
                contract()
            waiting.append((q, begin, end, (outer * inverse).astype(jnp.bfloat16)))
        for item, query, block_rows in extra:
            acc_ref[query, :, begin:end] += jnp.dot(
                block_rows, stored_ref[item, :, begin:end], preferred_element_type=jnp.float32
            )
    while waiting:
        contract()

    @pl.when(step == pl.num_programs(0) - 1)
    def _():
        start = 0
        for ref, score_ref in zip(token_refs, score_refs):
            stop = start + ref.shape[0]
            inside = ref[:, row_width:].astype(jnp.float32)
            for q in range(queries):
                score_ref[q, :] = jnp.sum(acc_ref[q, start:stop, :] * inside, axis=1)
            start = stop


def pick(total, unit, limit):
    best = total
    if total % unit == 0:
        for size in range(unit, min(total, limit) + 1, unit):
            if total % size == 0:
                best = size
    return best


def blocks_ahead(steps, queries):
    for ahead in range(1, steps // 2 + 1):
        if (ahead * queries) % (steps - ahead) == 0:
            return ahead
    return 0


def tile_scores(lam, query_out, query_in, received, row_tiles, col_tiles):
    rows, cols = lam.shape[1:]
    queries, depth = query_in.shape[:2]
    tokens = sum(part.shape[0] for part in received)
    height = pick(rows, 128, 256)
    steps = rows // height
    ahead = blocks_ahead(steps, queries)
    if cols % 128:
        col_part = lax.rem(lax.axis_index("cand"), col_tiles)
        query_in = lax.dynamic_slice_in_dim(query_in, col_part * cols, cols, 2)
    tiles = dict(row_tiles=row_tiles, col_tiles=col_tiles)
    operands = [lam, query_out, query_in, *received]
    specs = [
        pl.BlockSpec((1, height, cols), lambda i: (0, i + ahead, 0)),
        *[whole(array) for array in operands[1:]],
    ]
    if ahead:
        stored = pl.pallas_call(
            functools.partial(ahead_kernel, **tiles),
            grid=(ahead,),
            in_specs=[pl.BlockSpec((1, height, cols), lambda i: (0, i, 0)), *specs[1:3]],
            out_specs=pl.BlockSpec((queries, height, cols), lambda i: (i, 0, 0)),
            out_shape=jax.ShapeDtypeStruct((ahead * queries, height, cols), jnp.bfloat16),
            compiler_params=pltpu.CompilerParams(vmem_limit_bytes=GRANT_AHEAD),
            cost_estimate=pl.CostEstimate(
                flops=2 * queries * ahead * height * cols * 256,
                bytes_accessed=ahead * height * cols * 2 * (queries + 1),
                transcendentals=ahead * height * cols,
            ),
        )(*operands[:3])
        per = ahead * queries // (steps - ahead)
        operands.append(stored)
        specs.append(pl.BlockSpec((per, height, cols), lambda i: (i, 0, 0)))
    results = [jax.ShapeDtypeStruct((queries, part.shape[0]), jnp.float32) for part in received]
    return pl.pallas_call(
        functools.partial(score_kernel, ahead=ahead, tokens=tokens, results=len(results), **tiles),
        grid=(steps - ahead,),
        in_specs=specs,
        out_specs=[whole(result) for result in results],
        out_shape=results,
        scratch_shapes=[
            pltpu.VMEM((queries, tokens, cols), jnp.float32),
            pltpu.VMEM((tokens, rows), jnp.bfloat16),
        ],
        compiler_params=pltpu.CompilerParams(vmem_limit_bytes=GRANT_MAIN),
        cost_estimate=pl.CostEstimate(
            flops=2 * queries * rows * cols * 512,
            bytes_accessed=2 * rows * cols,
            transcendentals=rows * cols,
        ),
    )(*operands)


def exchange(array):
    return lax.all_to_all(array, "cand", split_axis=0, concat_axis=0, tiled=True)


def shifted(array, shift, devices):
    pairs = [(device, (device + shift) % devices) for device in range(devices)]
    return lax.ppermute(array, "cand", pairs)


def body(cand_out, cand_in, query_out, query_in, eigenvalues, slot_blocks, live_counts):
    tile_count = lax.axis_size("cand")
    row_tiles = min(8, max(2, tile_count // 8))
    col_tiles = tile_count // row_tiles
    tokens = cand_out.shape[1]
    slot_count = slot_blocks.shape[2]
    queries = query_out.shape[0]
    by_shift = tile_count <= MAX_SHIFTS

    packed = pack_tokens(
        cand_out, cand_in, slot_blocks, row_tiles, col_tiles, tile_count, by_shift
    )
    if by_shift:
        received = [packed[0]] + [
            shifted(packed[shift], shift, tile_count) for shift in range(1, tile_count)
        ]
    else:
        received = [exchange(packed[0]).reshape(-1, packed[0].shape[2])]
    parts = tile_scores(eigenvalues, query_out, query_in, received, row_tiles, col_tiles)
    if by_shift:
        total = parts[0]
        for shift in range(1, tile_count):
            total = total + shifted(parts[shift], -shift, tile_count)
    else:
        split = jnp.moveaxis(parts[0].reshape(queries, tile_count, -1), 1, 0)
        total = jnp.sum(exchange(split), axis=0)
    scores = total.reshape(queries, slot_count, tokens).sum(axis=2)
    position = lax.axis_index("cand")
    own_live = lax.dynamic_index_in_dim(live_counts[0], position, 0, keepdims=False)
    used = jnp.arange(slot_count, dtype=jnp.int32) < own_live
    return jnp.where(used[None], scores, 0.0)[:, None, :]


def solution(mesh):
    return jax.shard_map(
        body,
        mesh=mesh,
        in_specs=(
            P(("parts", "cand"), None, None),
            P(("parts", "cand"), None, None),
            P(("parts", "query"), None, None),
            P(("parts", "query"), None, None),
            P("cand", None, None),
            P(("parts", "query"), None, None),
            P(("parts", "query"), None),
        ),
        out_specs=P(("parts", "query"), "cand", None),
        check_vma=False,
    )
```

```python
import functools

import jax
import jax.numpy as jnp
from jax import lax
from jax.experimental import pallas as pl
from jax.experimental.pallas import tpu as pltpu
from jax.sharding import PartitionSpec as P

DAMPING = 0.05
PIECE = 512
BEHIND = 2
MAX_SHIFTS = 8
GRANT_PACK = 8 << 20


def pack_kernel(list_ref, out_ref, in_ref, *results, row_tiles, col_tiles, shifts, by_shift):
    position = lax.axis_index("cand")
    slots = list_ref.shape[1]
    tokens = out_ref.shape[1]
    row_width = out_ref.shape[2] // row_tiles
    col_width = in_ref.shape[2] // col_tiles

    def store(source, target, part, width, parts):
        for piece in range(parts):

            @pl.when(part == piece)
            def _():
                for slot in range(slots):
                    block = list_ref[0, slot, position]
                    target[slot * tokens : (slot + 1) * tokens, :] = source[
                        block, :, piece * width : (piece + 1) * width
                    ]

    for shift in range(shifts):
        if by_shift:
            tile = lax.rem(position + shift, shifts)
            targets = results[shift], results[shifts + shift]
        else:
            tile = jnp.int32(shift)
            targets = results[0].at[shift], results[1].at[shift]
        store(out_ref, targets[0], tile // col_tiles, row_width, row_tiles)
        store(in_ref, targets[1], lax.rem(tile, col_tiles), col_width, col_tiles)


def in_hbm(array):
    return pltpu.with_memory_space_constraint(array, pltpu.HBM)


def whole(array):
    return pl.BlockSpec(array.shape, lambda *i: (0,) * len(array.shape))


def pack_tokens(cand_out, cand_in, slot_blocks, row_tiles, col_tiles, shifts, by_shift):
    lists = jnp.swapaxes(slot_blocks, 1, 2)
    rows = slot_blocks.shape[2] * cand_out.shape[1]
    widths = cand_out.shape[2] // row_tiles, cand_in.shape[2] // col_tiles
    if by_shift:
        shapes = [(rows, width) for width in widths for _ in range(shifts)]
    else:
        shapes = [(shifts, rows, width) for width in widths]
    results = [jax.ShapeDtypeStruct(shape, cand_out.dtype) for shape in shapes]
    return pl.pallas_call(
        functools.partial(
            pack_kernel,
            row_tiles=row_tiles,
            col_tiles=col_tiles,
            shifts=shifts,
            by_shift=by_shift,
        ),
        grid=(1,),
        in_specs=[pl.BlockSpec(memory_space=pltpu.SMEM), whole(cand_out), whole(cand_in)],
        out_specs=[whole(result) for result in results],
        out_shape=results,
        compiler_params=pltpu.CompilerParams(vmem_limit_bytes=GRANT_PACK),
    )(in_hbm(lists), in_hbm(cand_out), in_hbm(cand_in))


class Factors:
    def __init__(self, left_ref, right_ref, height, cols, row_tiles, col_tiles):
        position = lax.axis_index("cand")
        self.left_ref, self.right_ref = left_ref, right_ref
        self.height, self.cols = height, cols
        self.row_start = (position // col_tiles) * (left_ref.shape[2] // row_tiles)
        self.split = right_ref.shape[2] != cols
        self.col_start = lax.rem(position, col_tiles) * cols

    def left(self, query, block):
        start = pl.multiple_of(self.row_start + block * self.height, 128)
        rows = self.left_ref[query, :, pl.ds(start, self.height)]
        return rows.astype(jnp.float32).T.astype(jnp.bfloat16)

    def right(self, query, begin, end):
        if not self.split:
            return self.right_ref[query, :, begin:end]
        start = pl.multiple_of(self.col_start + begin, 128)
        return self.right_ref[query, :, pl.ds(start, end - begin)]


def map_kernel(lam_ref, left_ref, right_ref, *refs, row_tiles, col_tiles):
    token_refs, acc_ref, token_buf = refs[:-2], refs[-2], refs[-1]
    queries, height, cols = left_ref.shape[0], lam_ref.shape[1], lam_ref.shape[2]
    step = pl.program_id(0)

    @pl.when(step == 0)
    def _():
        acc_ref[...] = jnp.zeros_like(acc_ref)
        start = 0
        for ref in token_refs:
            token_buf[start : start + ref.shape[0], :] = ref[...]
            start += ref.shape[0]

    factors = Factors(left_ref, right_ref, height, cols, row_tiles, col_tiles)
    lefts = [factors.left(q, step) for q in range(queries)]
    rows = token_buf[:, pl.ds(pl.multiple_of(step * height, 128), height)]
    waiting = []

    def contract():
        q, begin, end, precond = waiting.pop(0)
        acc_ref[q, :, begin:end] += jnp.dot(rows, precond, preferred_element_type=jnp.float32)

    for begin in range(0, cols, PIECE):
        end = min(begin + PIECE, cols)
        inverse = 1.0 / (lam_ref[0, :, begin:end].astype(jnp.float32) + DAMPING)
        for q in range(queries):
            outer = jnp.dot(
                lefts[q], factors.right(q, begin, end), preferred_element_type=jnp.float32
            )
            if len(waiting) >= BEHIND:
                contract()
            waiting.append((q, begin, end, (outer * inverse).astype(jnp.bfloat16)))
    while waiting:
        contract()


def pick(total, unit, limit):
    best = total
    if total % unit == 0:
        for size in range(unit, min(total, limit) + 1, unit):
            if total % size == 0:
                best = size
    return best


def map_tokens(lam, query_out, query_in, out_tokens, row_tiles, col_tiles):
    rows, cols = lam.shape[1:]
    queries, depth = query_in.shape[:2]
    tokens = sum(part.shape[0] for part in out_tokens)
    height = pick(rows, 128, 256)
    if cols % 128:
        col_part = lax.rem(lax.axis_index("cand"), col_tiles)
        query_in = lax.dynamic_slice_in_dim(query_in, col_part * cols, cols, 2)
    grant = (16 << 20) + 4 * queries * tokens * cols + 4 * height * cols
    resident = pl.BlockSpec(memory_space=pltpu.VMEM)
    return pl.pallas_call(
        functools.partial(map_kernel, row_tiles=row_tiles, col_tiles=col_tiles),
        grid=(rows // height,),
        in_specs=[
            pl.BlockSpec((1, height, cols), lambda i: (0, i, 0)),
            whole(query_out),
            whole(query_in),
            *[resident] * len(out_tokens),
        ],
        out_specs=resident,
        out_shape=jax.ShapeDtypeStruct((queries, tokens, cols), jnp.float32),
        scratch_shapes=[pltpu.VMEM((tokens, rows), jnp.bfloat16)],
        compiler_params=pltpu.CompilerParams(vmem_limit_bytes=grant),
        cost_estimate=pl.CostEstimate(
            flops=2 * queries * rows * cols * 512,
            bytes_accessed=2 * rows * cols,
            transcendentals=rows * cols,
        ),
    )(lam, in_hbm(query_out), in_hbm(query_in), *out_tokens)


def fold_kernel(live_ref, mapped_ref, *refs, sources, per_slot):
    half = len(refs) // 2
    position = lax.axis_index("cand")
    start = 0
    for shift, (in_ref, score_ref) in enumerate(zip(refs[:half], refs[half:])):
        stop = start + in_ref.shape[0]
        inside = in_ref[...].astype(jnp.float32)
        for q in range(mapped_ref.shape[0]):
            score_ref[q, :] = jnp.sum(mapped_ref[q, start:stop, :] * inside, axis=1)
        start = stop
        if half == sources:
            live = live_ref[0, lax.rem(position + sources - shift, sources)]
            slot = lax.broadcasted_iota(jnp.int32, score_ref.shape, 1) // per_slot
            score_ref[...] = jnp.where(slot < live, score_ref[...], 0.0)


def fold_tokens(live_counts, mapped, in_tokens, per_slot):
    queries, tokens, cols = mapped.shape
    sources = live_counts.shape[1]
    grant = min((8 << 20) + 12 * queries * tokens * cols, 60 << 20)
    resident = pl.BlockSpec(memory_space=pltpu.VMEM)
    results = [jax.ShapeDtypeStruct((queries, part.shape[0]), jnp.float32) for part in in_tokens]
    return pl.pallas_call(
        functools.partial(fold_kernel, sources=sources, per_slot=per_slot),
        in_specs=[pl.BlockSpec(memory_space=pltpu.SMEM)] + [resident] * (1 + len(in_tokens)),
        out_specs=[resident] * len(results),
        out_shape=results,
        compiler_params=pltpu.CompilerParams(vmem_limit_bytes=grant),
    )(in_hbm(live_counts), mapped, *in_tokens)


def exchange(array):
    return lax.all_to_all(array, "cand", split_axis=0, concat_axis=0, tiled=True)


def shifted(array, shift, devices):
    pairs = [(device, (device + shift) % devices) for device in range(devices)]
    return lax.ppermute(array, "cand", pairs)


def body(cand_out, cand_in, query_out, query_in, eigenvalues, slot_blocks, live_counts):
    tile_count = lax.axis_size("cand")
    row_tiles = min(8, max(2, tile_count // 8))
    col_tiles = tile_count // row_tiles
    tokens = cand_out.shape[1]
    slot_count = slot_blocks.shape[2]
    queries = query_out.shape[0]
    by_shift = tile_count <= MAX_SHIFTS

    packed = pack_tokens(
        cand_out, cand_in, slot_blocks, row_tiles, col_tiles, tile_count, by_shift
    )
    if by_shift:
        out_tokens, in_tokens = [
            [group[0]] + [shifted(group[s], s, tile_count) for s in range(1, tile_count)]
            for group in (packed[:tile_count], packed[tile_count:])
        ]
    else:
        out_tokens, in_tokens = [
            [exchange(group).reshape(-1, group.shape[2])] for group in packed
        ]
    mapped = map_tokens(eigenvalues, query_out, query_in, out_tokens, row_tiles, col_tiles)
    parts = fold_tokens(live_counts, mapped, in_tokens, tokens)
    if by_shift:
        total = parts[0]
        for shift in range(1, tile_count):
            total = total + shifted(parts[shift], -shift, tile_count)
        return total.reshape(queries, 1, slot_count, tokens).sum(axis=3)
    split = jnp.moveaxis(parts[0].reshape(queries, tile_count, -1), 1, 0)
    total = jnp.sum(exchange(split), axis=0)
    scores = total.reshape(queries, slot_count, tokens).sum(axis=2)
    position = lax.axis_index("cand")
    own_live = lax.dynamic_index_in_dim(live_counts[0], position, 0, keepdims=False)
    used = jnp.arange(slot_count, dtype=jnp.int32) < own_live
    return jnp.where(used[None], scores, 0.0)[:, None, :]


def solution(mesh):
    return jax.shard_map(
        body,
        mesh=mesh,
        in_specs=(
            P(("parts", "cand"), None, None),
            P(("parts", "cand"), None, None),
            P(("parts", "query"), None, None),
            P(("parts", "query"), None, None),
            P("cand", None, None),
            P(("parts", "query"), None, None),
            P(("parts", "query"), None),
        ),
        out_specs=P(("parts", "query"), "cand", None),
        check_vma=False,
    )
```

```python
import functools

import jax
import jax.numpy as jnp
from jax import lax
from jax.experimental import pallas as pl
from jax.experimental.pallas import tpu as pltpu
from jax.sharding import PartitionSpec as P

DAMPING = 0.05
PIECE = 512
BEHIND = 2
GRANT_PACK = 8 << 20


def pack_kernel(list_ref, out_ref, in_ref, *results, row_tiles, col_tiles, shifts, paired):
    position = lax.axis_index("cand")
    slots = list_ref.shape[1]
    tokens = out_ref.shape[1]
    row_width = out_ref.shape[2] // row_tiles
    col_width = in_ref.shape[2] // col_tiles

    def store(source, target, part, width, parts):
        for piece in range(parts):

            @pl.when(part == piece)
            def _():
                for slot in range(slots):
                    block = list_ref[0, slot, position]
                    target[slot * tokens : (slot + 1) * tokens, :] = source[
                        block, :, piece * width : (piece + 1) * width
                    ]

    for shift in range(shifts):
        if paired:
            tile = lax.bitwise_xor(position, jnp.int32(shift))
            targets = results[shift], results[shifts + shift]
        else:
            tile = jnp.int32(shift)
            targets = results[0].at[shift], results[1].at[shift]
        store(out_ref, targets[0], tile // col_tiles, row_width, row_tiles)
        store(in_ref, targets[1], lax.rem(tile, col_tiles), col_width, col_tiles)


def in_hbm(array):
    return pltpu.with_memory_space_constraint(array, pltpu.HBM)


def whole(array):
    return pl.BlockSpec(array.shape, lambda *i: (0,) * len(array.shape))


def pack_tokens(cand_out, cand_in, slot_blocks, row_tiles, col_tiles, shifts, paired):
    lists = jnp.swapaxes(slot_blocks, 1, 2)
    rows = slot_blocks.shape[2] * cand_out.shape[1]
    widths = cand_out.shape[2] // row_tiles, cand_in.shape[2] // col_tiles
    if paired:
        shapes = [(rows, width) for width in widths for _ in range(shifts)]
    else:
        shapes = [(shifts, rows, width) for width in widths]
    results = [jax.ShapeDtypeStruct(shape, cand_out.dtype) for shape in shapes]
    return pl.pallas_call(
        functools.partial(
            pack_kernel,
            row_tiles=row_tiles,
            col_tiles=col_tiles,
            shifts=shifts,
            paired=paired,
        ),
        grid=(1,),
        in_specs=[pl.BlockSpec(memory_space=pltpu.SMEM), whole(cand_out), whole(cand_in)],
        out_specs=[whole(result) for result in results],
        out_shape=results,
        compiler_params=pltpu.CompilerParams(vmem_limit_bytes=GRANT_PACK),
    )(in_hbm(lists), in_hbm(cand_out), in_hbm(cand_in))


class Factors:
    def __init__(self, left_ref, right_ref, height, cols, row_tiles, col_tiles):
        position = lax.axis_index("cand")
        self.left_ref, self.right_ref = left_ref, right_ref
        self.height, self.cols = height, cols
        self.row_start = (position // col_tiles) * (left_ref.shape[2] // row_tiles)
        self.split = right_ref.shape[2] != cols
        self.col_start = lax.rem(position, col_tiles) * cols

    def left(self, query, block):
        start = pl.multiple_of(self.row_start + block * self.height, 128)
        rows = self.left_ref[query, :, pl.ds(start, self.height)]
        return rows.astype(jnp.float32).T.astype(jnp.bfloat16)

    def right(self, query, begin, end):
        if not self.split:
            return self.right_ref[query, :, begin:end]
        start = pl.multiple_of(self.col_start + begin, 128)
        return self.right_ref[query, :, pl.ds(start, end - begin)]


def map_kernel(lam_ref, left_ref, right_ref, *refs, row_tiles, col_tiles):
    token_refs, acc_ref, token_buf = refs[:-2], refs[-2], refs[-1]
    queries, height, cols = left_ref.shape[0], lam_ref.shape[1], lam_ref.shape[2]
    step = pl.program_id(0)

    @pl.when(step == 0)
    def _():
        acc_ref[...] = jnp.zeros_like(acc_ref)
        start = 0
        for ref in token_refs:
            token_buf[start : start + ref.shape[0], :] = ref[...]
            start += ref.shape[0]

    factors = Factors(left_ref, right_ref, height, cols, row_tiles, col_tiles)
    lefts = [factors.left(q, step) for q in range(queries)]
    rows = token_buf[:, pl.ds(pl.multiple_of(step * height, 128), height)]
    waiting = []

    def contract():
        q, begin, end, precond = waiting.pop(0)
        acc_ref[q, :, begin:end] += jnp.dot(rows, precond, preferred_element_type=jnp.float32)

    for begin in range(0, cols, PIECE):
        end = min(begin + PIECE, cols)
        inverse = 1.0 / (lam_ref[0, :, begin:end].astype(jnp.float32) + DAMPING)
        for q in range(queries):
            outer = jnp.dot(
                lefts[q], factors.right(q, begin, end), preferred_element_type=jnp.float32
            )
            if len(waiting) >= BEHIND:
                contract()
            waiting.append((q, begin, end, (outer * inverse).astype(jnp.bfloat16)))
    while waiting:
        contract()


def pick(total, unit, limit):
    best = total
    if total % unit == 0:
        for size in range(unit, min(total, limit) + 1, unit):
            if total % size == 0:
                best = size
    return best


def map_tokens(lam, query_out, query_in, out_tokens, row_tiles, col_tiles):
    rows, cols = lam.shape[1:]
    queries, depth = query_in.shape[:2]
    tokens = sum(part.shape[0] for part in out_tokens)
    height = pick(rows, 128, 256)
    if cols % 128:
        col_part = lax.rem(lax.axis_index("cand"), col_tiles)
        query_in = lax.dynamic_slice_in_dim(query_in, col_part * cols, cols, 2)
    grant = (16 << 20) + 4 * queries * tokens * cols + 4 * height * cols
    resident = pl.BlockSpec(memory_space=pltpu.VMEM)
    return pl.pallas_call(
        functools.partial(map_kernel, row_tiles=row_tiles, col_tiles=col_tiles),
        grid=(rows // height,),
        in_specs=[
            pl.BlockSpec((1, height, cols), lambda i: (0, i, 0)),
            whole(query_out),
            whole(query_in),
            *[resident] * len(out_tokens),
        ],
        out_specs=resident,
        out_shape=jax.ShapeDtypeStruct((queries, tokens, cols), jnp.float32),
        scratch_shapes=[pltpu.VMEM((tokens, rows), jnp.bfloat16)],
        compiler_params=pltpu.CompilerParams(vmem_limit_bytes=grant),
        cost_estimate=pl.CostEstimate(
            flops=2 * queries * rows * cols * 512,
            bytes_accessed=2 * rows * cols,
            transcendentals=rows * cols,
        ),
    )(lam, in_hbm(query_out), in_hbm(query_in), *out_tokens)


def fold_kernel(live_ref, mapped_ref, *refs, paired, per_slot):
    queries = mapped_ref.shape[0]
    token_refs = refs[:-2] if paired else refs[:-1]
    position = lax.axis_index("cand")
    start = 0
    for index, in_ref in enumerate(token_refs):
        rows = in_ref.shape[0]
        inside = in_ref[...].astype(jnp.float32)
        sums = [
            jnp.sum(mapped_ref[q, start : start + rows, :] * inside, axis=1, keepdims=True)
            for q in range(queries)
        ]
        start += rows
        if not paired:
            for q in range(queries):
                refs[-1][q, :] = sums[q][:, 0]
            continue
        lane = lax.broadcasted_iota(jnp.int32, (rows, queries), 1)
        table = sum(jnp.where(lane == q, sums[q], 0.0) for q in range(queries))
        live = live_ref[0, lax.bitwise_xor(position, jnp.int32(index))]
        half = len(token_refs) // 2
        target = refs[-2 + index // half]
        for slot in range(rows // per_slot):
            part = table[slot * per_slot : (slot + 1) * per_slot]
            total = jnp.sum(part, axis=0, keepdims=True)
            target[index % half, slot : slot + 1, :] = jnp.where(slot < live, total, 0.0)


def fold_tokens(live_counts, mapped, in_tokens, per_slot, paired):
    queries, tokens, cols = mapped.shape
    grant = min((8 << 20) + 12 * queries * tokens * cols, 60 << 20)
    resident = pl.BlockSpec(memory_space=pltpu.VMEM)
    if paired:
        shape = (len(in_tokens) // 2, in_tokens[0].shape[0] // per_slot, queries)
        results = [jax.ShapeDtypeStruct(shape, jnp.float32)] * 2
    else:
        results = [jax.ShapeDtypeStruct((queries, tokens), jnp.float32)]
    return pl.pallas_call(
        functools.partial(fold_kernel, paired=paired, per_slot=per_slot),
        in_specs=[pl.BlockSpec(memory_space=pltpu.SMEM)] + [resident] * (1 + len(in_tokens)),
        out_specs=[resident] * len(results),
        out_shape=results,
        compiler_params=pltpu.CompilerParams(vmem_limit_bytes=grant),
    )(in_hbm(live_counts), mapped, *in_tokens)


def exchange(array):
    return lax.all_to_all(array, "cand", split_axis=0, concat_axis=0, tiled=True)


def swapped(array, bit, devices):
    pairs = [(device, device ^ bit) for device in range(devices)]
    return lax.ppermute(array, "cand", pairs)


def body(cand_out, cand_in, query_out, query_in, eigenvalues, slot_blocks, live_counts):
    tile_count = lax.axis_size("cand")
    row_tiles = min(8, max(2, tile_count // 8))
    col_tiles = tile_count // row_tiles
    tokens = cand_out.shape[1]
    slot_count = slot_blocks.shape[2]
    queries = query_out.shape[0]
    paired = tile_count in (2, 4, 8)

    packed = pack_tokens(
        cand_out, cand_in, slot_blocks, row_tiles, col_tiles, tile_count, paired
    )
    if paired:
        out_tokens, in_tokens = [
            [group[0]] + [swapped(group[s], s, tile_count) for s in range(1, tile_count)]
            for group in (packed[:tile_count], packed[tile_count:])
        ]
    else:
        out_tokens, in_tokens = [
            [exchange(group).reshape(-1, group.shape[2])] for group in packed
        ]
    mapped = map_tokens(eigenvalues, query_out, query_in, out_tokens, row_tiles, col_tiles)
    parts = fold_tokens(live_counts, mapped, in_tokens, tokens, paired)
    if paired:
        kept, sent = parts
        bit = tile_count // 2
        while True:
            kept = kept + swapped(sent, bit, tile_count)
            bit //= 2
            if not bit:
                return jnp.transpose(kept, (2, 0, 1))
            kept, sent = kept[:bit], kept[bit:]
    split = jnp.moveaxis(parts[0].reshape(queries, tile_count, -1), 1, 0)
    total = jnp.sum(exchange(split), axis=0)
    scores = total.reshape(queries, slot_count, tokens).sum(axis=2)
    position = lax.axis_index("cand")
    own_live = lax.dynamic_index_in_dim(live_counts[0], position, 0, keepdims=False)
    used = jnp.arange(slot_count, dtype=jnp.int32) < own_live
    return jnp.where(used[None], scores, 0.0)[:, None, :]


def solution(mesh):
    return jax.shard_map(
        body,
        mesh=mesh,
        in_specs=(
            P(("parts", "cand"), None, None),
            P(("parts", "cand"), None, None),
            P(("parts", "query"), None, None),
            P(("parts", "query"), None, None),
            P("cand", None, None),
            P(("parts", "query"), None, None),
            P(("parts", "query"), None),
        ),
        out_specs=P(("parts", "query"), "cand", None),
        check_vma=False,
    )
```

```python
import functools

import jax
import jax.numpy as jnp
from jax import lax
from jax.experimental import pallas as pl
from jax.experimental.pallas import tpu as pltpu
from jax.sharding import PartitionSpec as P

DAMPING = 0.05
PIECE = 512
BEHIND = 2
MAX_SHIFTS = 8
GRANT_PACK = 8 << 20


def pack_kernel(list_ref, out_ref, in_ref, *results, row_tiles, col_tiles, shifts, by_shift):
    position = lax.axis_index("cand")
    slots = list_ref.shape[1]
    tokens = out_ref.shape[1]
    row_width = out_ref.shape[2] // row_tiles
    col_width = in_ref.shape[2] // col_tiles

    def store(source, target, part, width, parts):
        for piece in range(parts):

            @pl.when(part == piece)
            def _():
                for slot in range(slots):
                    block = list_ref[0, slot, position]
                    target[slot * tokens : (slot + 1) * tokens, :] = source[
                        block, :, piece * width : (piece + 1) * width
                    ]

    for shift in range(shifts):
        if by_shift:
            tile = lax.rem(position + shift, shifts)
            targets = results[shift], results[shifts + shift]
        else:
            tile = jnp.int32(shift)
            targets = results[0].at[shift], results[1].at[shift]
        store(out_ref, targets[0], tile // col_tiles, row_width, row_tiles)
        store(in_ref, targets[1], lax.rem(tile, col_tiles), col_width, col_tiles)


def in_hbm(array):
    return pltpu.with_memory_space_constraint(array, pltpu.HBM)


def whole(array):
    return pl.BlockSpec(array.shape, lambda *i: (0,) * len(array.shape))


def pack_tokens(cand_out, cand_in, slot_blocks, row_tiles, col_tiles, shifts, by_shift):
    lists = jnp.swapaxes(slot_blocks, 1, 2)
    rows = slot_blocks.shape[2] * cand_out.shape[1]
    widths = cand_out.shape[2] // row_tiles, cand_in.shape[2] // col_tiles
    if by_shift:
        shapes = [(rows, width) for width in widths for _ in range(shifts)]
    else:
        shapes = [(shifts, rows, width) for width in widths]
    results = [jax.ShapeDtypeStruct(shape, cand_out.dtype) for shape in shapes]
    return pl.pallas_call(
        functools.partial(
            pack_kernel,
            row_tiles=row_tiles,
            col_tiles=col_tiles,
            shifts=shifts,
            by_shift=by_shift,
        ),
        grid=(1,),
        in_specs=[pl.BlockSpec(memory_space=pltpu.SMEM), whole(cand_out), whole(cand_in)],
        out_specs=[whole(result) for result in results],
        out_shape=results,
        compiler_params=pltpu.CompilerParams(vmem_limit_bytes=GRANT_PACK),
    )(in_hbm(lists), in_hbm(cand_out), in_hbm(cand_in))


class Factors:
    def __init__(self, left_ref, right_ref, height, cols, row_tiles, col_tiles):
        position = lax.axis_index("cand")
        self.left_ref, self.right_ref = left_ref, right_ref
        self.height, self.cols = height, cols
        self.row_start = (position // col_tiles) * (left_ref.shape[2] // row_tiles)
        self.split = right_ref.shape[2] != cols
        self.col_start = lax.rem(position, col_tiles) * cols

    def left(self, query, block):
        start = pl.multiple_of(self.row_start + block * self.height, 128)
        rows = self.left_ref[query, :, pl.ds(start, self.height)]
        return rows.astype(jnp.float32).T.astype(jnp.bfloat16)

    def right(self, query, begin, end):
        if not self.split:
            return self.right_ref[query, :, begin:end]
        start = pl.multiple_of(self.col_start + begin, 128)
        return self.right_ref[query, :, pl.ds(start, end - begin)]


def map_kernel(lam_ref, left_ref, right_ref, *refs, row_tiles, col_tiles):
    token_refs, acc_ref, token_buf = refs[:-2], refs[-2], refs[-1]
    queries, height, cols = left_ref.shape[0], lam_ref.shape[1], lam_ref.shape[2]
    step = pl.program_id(0)

    @pl.when(step == 0)
    def _():
        acc_ref[...] = jnp.zeros_like(acc_ref)
        start = 0
        for ref in token_refs:
            token_buf[start : start + ref.shape[0], :] = ref[...]
            start += ref.shape[0]

    factors = Factors(left_ref, right_ref, height, cols, row_tiles, col_tiles)
    lefts = [factors.left(q, step) for q in range(queries)]
    rows = token_buf[:, pl.ds(pl.multiple_of(step * height, 128), height)]
    waiting = []

    def contract():
        q, begin, end, precond = waiting.pop(0)
        acc_ref[q, :, begin:end] += jnp.dot(rows, precond, preferred_element_type=jnp.float32)

    for begin in range(0, cols, PIECE):
        end = min(begin + PIECE, cols)
        inverse = 1.0 / (lam_ref[0, :, begin:end].astype(jnp.float32) + DAMPING)
        for q in range(queries):
            outer = jnp.dot(
                lefts[q], factors.right(q, begin, end), preferred_element_type=jnp.float32
            )
            if len(waiting) >= BEHIND:
                contract()
            waiting.append((q, begin, end, (outer * inverse).astype(jnp.bfloat16)))
    while waiting:
        contract()


def pick(total, unit, limit):
    best = total
    if total % unit == 0:
        for size in range(unit, min(total, limit) + 1, unit):
            if total % size == 0:
                best = size
    return best


def map_tokens(lam, query_out, query_in, out_tokens, row_tiles, col_tiles):
    rows, cols = lam.shape[1:]
    queries, depth = query_in.shape[:2]
    tokens = sum(part.shape[0] for part in out_tokens)
    height = pick(rows, 128, 256)
    if cols % 128:
        col_part = lax.rem(lax.axis_index("cand"), col_tiles)
        query_in = lax.dynamic_slice_in_dim(query_in, col_part * cols, cols, 2)
    grant = (16 << 20) + 4 * queries * tokens * cols + 4 * height * cols
    resident = pl.BlockSpec(memory_space=pltpu.VMEM)
    return pl.pallas_call(
        functools.partial(map_kernel, row_tiles=row_tiles, col_tiles=col_tiles),
        grid=(rows // height,),
        in_specs=[
            pl.BlockSpec((1, height, cols), lambda i: (0, i, 0)),
            whole(query_out),
            whole(query_in),
            *[resident] * len(out_tokens),
        ],
        out_specs=resident,
        out_shape=jax.ShapeDtypeStruct((queries, tokens, cols), jnp.float32),
        scratch_shapes=[pltpu.VMEM((tokens, rows), jnp.bfloat16)],
        compiler_params=pltpu.CompilerParams(vmem_limit_bytes=grant),
        cost_estimate=pl.CostEstimate(
            flops=2 * queries * rows * cols * 512,
            bytes_accessed=2 * rows * cols,
            transcendentals=rows * cols,
        ),
    )(lam, in_hbm(query_out), in_hbm(query_in), *out_tokens)


def fold_kernel(live_ref, mapped_ref, *refs, by_shift, per_slot):
    queries = mapped_ref.shape[0]
    token_refs = refs[: len(refs) // 2]
    position = lax.axis_index("cand")
    start = 0
    for index, in_ref in enumerate(token_refs):
        rows = in_ref.shape[0]
        inside = in_ref[...].astype(jnp.float32)
        sums = [
            jnp.sum(mapped_ref[q, start : start + rows, :] * inside, axis=1, keepdims=True)
            for q in range(queries)
        ]
        start += rows
        if not by_shift:
            for q in range(queries):
                refs[-1][q, :] = sums[q][:, 0]
            continue
        lane = lax.broadcasted_iota(jnp.int32, (rows, queries), 1)
        table = sum(jnp.where(lane == q, sums[q], 0.0) for q in range(queries))
        sources = len(token_refs)
        live = live_ref[0, lax.rem(position + sources - index, sources)]
        target = refs[sources + index]
        for slot in range(rows // per_slot):
            part = table[slot * per_slot : (slot + 1) * per_slot]
            total = jnp.sum(part, axis=0, keepdims=True)
            target[slot : slot + 1, :] = jnp.where(slot < live, total, 0.0)


def fold_tokens(live_counts, mapped, in_tokens, per_slot, by_shift):
    queries, tokens, cols = mapped.shape
    grant = min((8 << 20) + 12 * queries * tokens * cols, 60 << 20)
    resident = pl.BlockSpec(memory_space=pltpu.VMEM)
    if by_shift:
        shape = (in_tokens[0].shape[0] // per_slot, queries)
        results = [jax.ShapeDtypeStruct(shape, jnp.float32)] * len(in_tokens)
    else:
        results = [jax.ShapeDtypeStruct((queries, tokens), jnp.float32)]
    return pl.pallas_call(
        functools.partial(fold_kernel, by_shift=by_shift, per_slot=per_slot),
        in_specs=[pl.BlockSpec(memory_space=pltpu.SMEM)] + [resident] * (1 + len(in_tokens)),
        out_specs=[resident] * len(results),
        out_shape=results,
        compiler_params=pltpu.CompilerParams(vmem_limit_bytes=grant),
    )(in_hbm(live_counts), mapped, *in_tokens)


def exchange(array):
    return lax.all_to_all(array, "cand", split_axis=0, concat_axis=0, tiled=True)


def shifted(array, shift, devices):
    pairs = [(device, (device + shift) % devices) for device in range(devices)]
    return lax.ppermute(array, "cand", pairs)


def body(cand_out, cand_in, query_out, query_in, eigenvalues, slot_blocks, live_counts):
    tile_count = lax.axis_size("cand")
    row_tiles = min(8, max(2, tile_count // 8))
    col_tiles = tile_count // row_tiles
    tokens = cand_out.shape[1]
    slot_count = slot_blocks.shape[2]
    queries = query_out.shape[0]
    by_shift = tile_count <= MAX_SHIFTS

    packed = pack_tokens(
        cand_out, cand_in, slot_blocks, row_tiles, col_tiles, tile_count, by_shift
    )
    if by_shift:
        out_tokens, in_tokens = [
            [group[0]] + [shifted(group[s], s, tile_count) for s in range(1, tile_count)]
            for group in (packed[:tile_count], packed[tile_count:])
        ]
    else:
        out_tokens, in_tokens = [
            [exchange(group).reshape(-1, group.shape[2])] for group in packed
        ]
    mapped = map_tokens(eigenvalues, query_out, query_in, out_tokens, row_tiles, col_tiles)
    parts = fold_tokens(live_counts, mapped, in_tokens, tokens, by_shift)
    if by_shift:
        total = parts[0]
        for shift in range(1, tile_count):
            total = total + shifted(parts[shift], -shift, tile_count)
        return jnp.transpose(total[None], (2, 0, 1))
    split = jnp.moveaxis(parts[0].reshape(queries, tile_count, -1), 1, 0)
    total = jnp.sum(exchange(split), axis=0)
    scores = total.reshape(queries, slot_count, tokens).sum(axis=2)
    position = lax.axis_index("cand")
    own_live = lax.dynamic_index_in_dim(live_counts[0], position, 0, keepdims=False)
    used = jnp.arange(slot_count, dtype=jnp.int32) < own_live
    return jnp.where(used[None], scores, 0.0)[:, None, :]


def solution(mesh):
    return jax.shard_map(
        body,
        mesh=mesh,
        in_specs=(
            P(("parts", "cand"), None, None),
            P(("parts", "cand"), None, None),
            P(("parts", "query"), None, None),
            P(("parts", "query"), None, None),
            P("cand", None, None),
            P(("parts", "query"), None, None),
            P(("parts", "query"), None),
        ),
        out_specs=P(("parts", "query"), "cand", None),
        check_vma=False,
    )
```

```python
import functools

import jax
import jax.numpy as jnp
from jax import lax
from jax.experimental import pallas as pl
from jax.experimental.pallas import tpu as pltpu
from jax.sharding import PartitionSpec as P

DAMPING = 0.05
PIECE = 512
BEHIND = 2
MAX_SHIFTS = 8
GRANT_PACK = 8 << 20


def pack_kernel(list_ref, out_ref, in_ref, *results, row_tiles, col_tiles, shifts, by_shift):
    position = lax.axis_index("cand")
    slots = list_ref.shape[1]
    tokens = out_ref.shape[1]
    row_width = out_ref.shape[2] // row_tiles
    col_width = in_ref.shape[2] // col_tiles

    def store(source, target, part, width, parts):
        for piece in range(parts):

            @pl.when(part == piece)
            def _():
                for slot in range(slots):
                    block = list_ref[0, slot, position]
                    target[slot * tokens : (slot + 1) * tokens, :] = source[
                        block, :, piece * width : (piece + 1) * width
                    ]

    for shift in range(shifts):
        if by_shift:
            tile = lax.rem(position + shift, shifts)
            targets = results[shift], results[shifts + shift]
        else:
            tile = jnp.int32(shift)
            targets = results[0].at[shift], results[1].at[shift]
        store(out_ref, targets[0], tile // col_tiles, row_width, row_tiles)
        store(in_ref, targets[1], lax.rem(tile, col_tiles), col_width, col_tiles)


def in_hbm(array):
    return pltpu.with_memory_space_constraint(array, pltpu.HBM)


def whole(array):
    return pl.BlockSpec(array.shape, lambda *i: (0,) * len(array.shape))


def pack_tokens(cand_out, cand_in, slot_blocks, row_tiles, col_tiles, shifts, by_shift):
    lists = jnp.swapaxes(slot_blocks, 1, 2)
    rows = slot_blocks.shape[2] * cand_out.shape[1]
    widths = cand_out.shape[2] // row_tiles, cand_in.shape[2] // col_tiles
    if by_shift:
        shapes = [(rows, width) for width in widths for _ in range(shifts)]
    else:
        shapes = [(shifts, rows, width) for width in widths]
    results = [jax.ShapeDtypeStruct(shape, cand_out.dtype) for shape in shapes]
    return pl.pallas_call(
        functools.partial(
            pack_kernel,
            row_tiles=row_tiles,
            col_tiles=col_tiles,
            shifts=shifts,
            by_shift=by_shift,
        ),
        grid=(1,),
        in_specs=[pl.BlockSpec(memory_space=pltpu.SMEM), whole(cand_out), whole(cand_in)],
        out_specs=[whole(result) for result in results],
        out_shape=results,
        compiler_params=pltpu.CompilerParams(vmem_limit_bytes=GRANT_PACK),
    )(in_hbm(lists), in_hbm(cand_out), in_hbm(cand_in))


class Factors:
    def __init__(self, left_ref, right_ref, height, cols, row_tiles, col_tiles):
        position = lax.axis_index("cand")
        self.left_ref, self.right_ref = left_ref, right_ref
        self.height, self.cols = height, cols
        self.row_start = (position // col_tiles) * (left_ref.shape[2] // row_tiles)
        self.split = right_ref.shape[2] != cols
        self.col_start = lax.rem(position, col_tiles) * cols

    def left(self, query, block):
        start = pl.multiple_of(self.row_start + block * self.height, 128)
        rows = self.left_ref[query, :, pl.ds(start, self.height)]
        return rows.astype(jnp.float32).T.astype(jnp.bfloat16)

    def right(self, query, begin, end):
        if not self.split:
            return self.right_ref[query, :, begin:end]
        start = pl.multiple_of(self.col_start + begin, 128)
        return self.right_ref[query, :, pl.ds(start, end - begin)]


def map_kernel(lam_ref, left_ref, right_ref, *refs, row_tiles, col_tiles):
    token_refs, (acc_ref, token_buf, held) = refs[:-3], refs[-3:]
    queries, height, cols = left_ref.shape[0], lam_ref.shape[1], lam_ref.shape[2]
    step = pl.program_id(0)

    @pl.when(step == 0)
    def _():
        acc_ref[...] = jnp.zeros_like(acc_ref)
        held[...] = jnp.zeros_like(held)
        start = 0
        for ref in token_refs:
            token_buf[start : start + ref.shape[0], :] = ref[...]
            start += ref.shape[0]

    factors = Factors(left_ref, right_ref, height, cols, row_tiles, col_tiles)
    lefts = [factors.left(q, step) for q in range(queries)]
    behind = held.shape[0]
    pieces = [(begin, min(begin + PIECE, cols)) for begin in range(0, cols, PIECE)]
    begin, end = pieces[-1]

    def token_rows(block):
        return token_buf[:, pl.ds(pl.multiple_of(block * height, 128), height)]

    rows, rows_before = token_rows(step), token_rows(jnp.maximum(step - 1, 0))
    carried = range(queries - behind, queries)
    waiting = [
        (q, begin, end, rows_before, held[slot, :, : end - begin]) for slot, q in enumerate(carried)
    ]

    def contract():
        q, begin, end, mine, precond = waiting.pop(0)
        acc_ref[q, :, begin:end] += jnp.dot(mine, precond, preferred_element_type=jnp.float32)

    for begin, end in pieces:
        inverse = 1.0 / (lam_ref[0, :, begin:end].astype(jnp.float32) + DAMPING)
        for q in range(queries):
            outer = jnp.dot(
                lefts[q], factors.right(q, begin, end), preferred_element_type=jnp.float32
            )
            contract()
            waiting.append((q, begin, end, rows, (outer * inverse).astype(jnp.bfloat16)))
    for slot, item in enumerate(waiting):
        held[slot, :, : end - begin] = item[-1]

    @pl.when(step == pl.num_programs(0) - 1)
    def _():
        for slot, q in enumerate(carried):
            acc_ref[q, :, begin:end] += jnp.dot(
                rows, held[slot, :, : end - begin], preferred_element_type=jnp.float32
            )


def pick(total, unit, limit):
    best = total
    if total % unit == 0:
        for size in range(unit, min(total, limit) + 1, unit):
            if total % size == 0:
                best = size
    return best


def map_tokens(lam, query_out, query_in, out_tokens, row_tiles, col_tiles):
    rows, cols = lam.shape[1:]
    queries, depth = query_in.shape[:2]
    tokens = sum(part.shape[0] for part in out_tokens)
    height = pick(rows, 128, 256)
    if cols % 128:
        col_part = lax.rem(lax.axis_index("cand"), col_tiles)
        query_in = lax.dynamic_slice_in_dim(query_in, col_part * cols, cols, 2)
    grant = (16 << 20) + 4 * queries * tokens * cols + 4 * height * cols
    resident = pl.BlockSpec(memory_space=pltpu.VMEM)
    return pl.pallas_call(
        functools.partial(map_kernel, row_tiles=row_tiles, col_tiles=col_tiles),
        grid=(rows // height,),
        in_specs=[
            pl.BlockSpec((1, height, cols), lambda i: (0, i, 0)),
            whole(query_out),
            whole(query_in),
            *[resident] * len(out_tokens),
        ],
        out_specs=resident,
        out_shape=jax.ShapeDtypeStruct((queries, tokens, cols), jnp.float32),
        scratch_shapes=[
            pltpu.VMEM((tokens, rows), jnp.bfloat16),
            pltpu.VMEM((min(BEHIND, queries), height, min(PIECE, cols)), jnp.bfloat16),
        ],
        compiler_params=pltpu.CompilerParams(vmem_limit_bytes=grant),
        cost_estimate=pl.CostEstimate(
            flops=2 * queries * rows * cols * 512,
            bytes_accessed=2 * rows * cols,
            transcendentals=rows * cols,
        ),
    )(lam, in_hbm(query_out), in_hbm(query_in), *out_tokens)


def fold_kernel(live_ref, mapped_ref, *refs, by_shift, per_slot):
    queries = mapped_ref.shape[0]
    token_refs = refs[: len(refs) // 2]
    position = lax.axis_index("cand")
    start = 0
    for index, in_ref in enumerate(token_refs):
        rows = in_ref.shape[0]
        inside = in_ref[...].astype(jnp.float32)
        sums = [
            jnp.sum(mapped_ref[q, start : start + rows, :] * inside, axis=1, keepdims=True)
            for q in range(queries)
        ]
        start += rows
        if not by_shift:
            for q in range(queries):
                refs[-1][q, :] = sums[q][:, 0]
            continue
        lane = lax.broadcasted_iota(jnp.int32, (rows, queries), 1)
        table = sum(jnp.where(lane == q, sums[q], 0.0) for q in range(queries))
        sources = len(token_refs)
        live = live_ref[0, lax.rem(position + sources - index, sources)]
        target = refs[sources + index]
        for slot in range(rows // per_slot):
            part = table[slot * per_slot : (slot + 1) * per_slot]
            total = jnp.sum(part, axis=0, keepdims=True)
            target[slot : slot + 1, :] = jnp.where(slot < live, total, 0.0)


def fold_tokens(live_counts, mapped, in_tokens, per_slot, by_shift):
    queries, tokens, cols = mapped.shape
    grant = min((8 << 20) + 12 * queries * tokens * cols, 60 << 20)
    resident = pl.BlockSpec(memory_space=pltpu.VMEM)
    if by_shift:
        shape = (in_tokens[0].shape[0] // per_slot, queries)
        results = [jax.ShapeDtypeStruct(shape, jnp.float32)] * len(in_tokens)
    else:
        results = [jax.ShapeDtypeStruct((queries, tokens), jnp.float32)]
    return pl.pallas_call(
        functools.partial(fold_kernel, by_shift=by_shift, per_slot=per_slot),
        in_specs=[pl.BlockSpec(memory_space=pltpu.SMEM)] + [resident] * (1 + len(in_tokens)),
        out_specs=[resident] * len(results),
        out_shape=results,
        compiler_params=pltpu.CompilerParams(vmem_limit_bytes=grant),
    )(in_hbm(live_counts), mapped, *in_tokens)


def exchange(array):
    return lax.all_to_all(array, "cand", split_axis=0, concat_axis=0, tiled=True)


def shifted(array, shift, devices):
    pairs = [(device, (device + shift) % devices) for device in range(devices)]
    return lax.ppermute(array, "cand", pairs)


def body(cand_out, cand_in, query_out, query_in, eigenvalues, slot_blocks, live_counts):
    tile_count = lax.axis_size("cand")
    row_tiles = min(8, max(2, tile_count // 8))
    col_tiles = tile_count // row_tiles
    tokens = cand_out.shape[1]
    slot_count = slot_blocks.shape[2]
    queries = query_out.shape[0]
    by_shift = tile_count <= MAX_SHIFTS

    packed = pack_tokens(
        cand_out, cand_in, slot_blocks, row_tiles, col_tiles, tile_count, by_shift
    )
    if by_shift:
        out_tokens, in_tokens = [
            [group[0]] + [shifted(group[s], s, tile_count) for s in range(1, tile_count)]
            for group in (packed[:tile_count], packed[tile_count:])
        ]
    else:
        out_tokens, in_tokens = [
            [exchange(group).reshape(-1, group.shape[2])] for group in packed
        ]
    mapped = map_tokens(eigenvalues, query_out, query_in, out_tokens, row_tiles, col_tiles)
    parts = fold_tokens(live_counts, mapped, in_tokens, tokens, by_shift)
    if by_shift:
        total = parts[0]
        for shift in range(1, tile_count):
            total = total + shifted(parts[shift], -shift, tile_count)
        return jnp.transpose(total[None], (2, 0, 1))
    split = jnp.moveaxis(parts[0].reshape(queries, tile_count, -1), 1, 0)
    total = jnp.sum(exchange(split), axis=0)
    scores = total.reshape(queries, slot_count, tokens).sum(axis=2)
    position = lax.axis_index("cand")
    own_live = lax.dynamic_index_in_dim(live_counts[0], position, 0, keepdims=False)
    used = jnp.arange(slot_count, dtype=jnp.int32) < own_live
    return jnp.where(used[None], scores, 0.0)[:, None, :]


def solution(mesh):
    return jax.shard_map(
        body,
        mesh=mesh,
        in_specs=(
            P(("parts", "cand"), None, None),
            P(("parts", "cand"), None, None),
            P(("parts", "query"), None, None),
            P(("parts", "query"), None, None),
            P("cand", None, None),
            P(("parts", "query"), None, None),
            P(("parts", "query"), None),
        ),
        out_specs=P(("parts", "query"), "cand", None),
        check_vma=False,
    )
```

```python
import functools

import jax
import jax.numpy as jnp
from jax import lax
from jax.experimental import pallas as pl
from jax.experimental.pallas import tpu as pltpu
from jax.sharding import PartitionSpec as P

DAMPING = 0.05
PIECE = 512
BEHIND = 2
MAX_SHIFTS = 8
GRANT_PACK = 16 << 20


def pack_kernel(list_ref, out_ref, in_ref, *results, row_tiles, col_tiles, shifts, by_shift):
    position = lax.axis_index("cand")
    slots = list_ref.shape[1]
    tokens = out_ref.shape[1]
    row_width = out_ref.shape[2] // row_tiles
    col_width = in_ref.shape[2] // col_tiles

    def store(source, target, part, width, parts):
        for piece in range(parts):

            @pl.when(part == piece)
            def _():
                for slot in range(slots):
                    block = list_ref[0, slot, position]
                    target[slot * tokens : (slot + 1) * tokens, :] = source[
                        block, :, piece * width : (piece + 1) * width
                    ]

    for shift in range(shifts):
        if by_shift:
            tile = lax.rem(position + shift, shifts)
            targets = results[shift], results[shifts + shift]
        else:
            tile = jnp.int32(shift)
            targets = results[0].at[shift], results[1].at[shift]
        store(out_ref, targets[0], tile // col_tiles, row_width, row_tiles)
        store(in_ref, targets[1], lax.rem(tile, col_tiles), col_width, col_tiles)


def in_hbm(array):
    return pltpu.with_memory_space_constraint(array, pltpu.HBM)


def whole(array):
    return pl.BlockSpec(array.shape, lambda *i: (0,) * len(array.shape))


def pack_tokens(cand_out, cand_in, slot_blocks, row_tiles, col_tiles, shifts, by_shift):
    lists = jnp.swapaxes(slot_blocks, 1, 2)
    rows = slot_blocks.shape[2] * cand_out.shape[1]
    widths = cand_out.shape[2] // row_tiles, cand_in.shape[2] // col_tiles
    if by_shift:
        shapes = [(rows, width) for width in widths for _ in range(shifts)]
    else:
        shapes = [(shifts, rows, width) for width in widths]
    results = [jax.ShapeDtypeStruct(shape, cand_out.dtype) for shape in shapes]
    return pl.pallas_call(
        functools.partial(
            pack_kernel,
            row_tiles=row_tiles,
            col_tiles=col_tiles,
            shifts=shifts,
            by_shift=by_shift,
        ),
        grid=(1,),
        in_specs=[pl.BlockSpec(memory_space=pltpu.SMEM), whole(cand_out), whole(cand_in)],
        out_specs=[pl.BlockSpec(memory_space=pltpu.VMEM)] * len(results),
        out_shape=results,
        compiler_params=pltpu.CompilerParams(vmem_limit_bytes=GRANT_PACK),
    )(in_hbm(lists), in_hbm(cand_out), in_hbm(cand_in))


class Factors:
    def __init__(self, left_ref, right_ref, height, cols, row_tiles, col_tiles):
        position = lax.axis_index("cand")
        self.left_ref, self.right_ref = left_ref, right_ref
        self.height, self.cols = height, cols
        self.row_start = (position // col_tiles) * (left_ref.shape[2] // row_tiles)
        self.split = right_ref.shape[2] != cols
        self.col_start = lax.rem(position, col_tiles) * cols

    def left(self, query, block):
        start = pl.multiple_of(self.row_start + block * self.height, 128)
        rows = self.left_ref[query, :, pl.ds(start, self.height)]
        return rows.astype(jnp.float32).T.astype(jnp.bfloat16)

    def right(self, query, begin, end):
        if not self.split:
            return self.right_ref[query, :, begin:end]
        start = pl.multiple_of(self.col_start + begin, 128)
        return self.right_ref[query, :, pl.ds(start, end - begin)]


def map_kernel(lam_ref, left_ref, right_ref, *refs, row_tiles, col_tiles):
    token_refs, (acc_ref, token_buf, held) = refs[:-3], refs[-3:]
    queries, height, cols = left_ref.shape[0], lam_ref.shape[1], lam_ref.shape[2]
    step = pl.program_id(0)

    @pl.when(step == 0)
    def _():
        acc_ref[...] = jnp.zeros_like(acc_ref)
        held[...] = jnp.zeros_like(held)
        start = 0
        for ref in token_refs:
            token_buf[start : start + ref.shape[0], :] = ref[...]
            start += ref.shape[0]

    factors = Factors(left_ref, right_ref, height, cols, row_tiles, col_tiles)
    lefts = [factors.left(q, step) for q in range(queries)]
    behind = held.shape[0]
    pieces = [(begin, min(begin + PIECE, cols)) for begin in range(0, cols, PIECE)]
    begin, end = pieces[-1]

    def token_rows(block):
        return token_buf[:, pl.ds(pl.multiple_of(block * height, 128), height)]

    rows, rows_before = token_rows(step), token_rows(jnp.maximum(step - 1, 0))
    carried = range(queries - behind, queries)
    waiting = [
        (q, begin, end, rows_before, held[slot, :, : end - begin]) for slot, q in enumerate(carried)
    ]

    def contract():
        q, begin, end, mine, precond = waiting.pop(0)
        acc_ref[q, :, begin:end] += jnp.dot(mine, precond, preferred_element_type=jnp.float32)

    for begin, end in pieces:
        inverse = 1.0 / (lam_ref[0, :, begin:end].astype(jnp.float32) + DAMPING)
        for q in range(queries):
            outer = jnp.dot(
                lefts[q], factors.right(q, begin, end), preferred_element_type=jnp.float32
            )
            contract()
            waiting.append((q, begin, end, rows, (outer * inverse).astype(jnp.bfloat16)))
    for slot, item in enumerate(waiting):
        held[slot, :, : end - begin] = item[-1]

    @pl.when(step == pl.num_programs(0) - 1)
    def _():
        for slot, q in enumerate(carried):
            acc_ref[q, :, begin:end] += jnp.dot(
                rows, held[slot, :, : end - begin], preferred_element_type=jnp.float32
            )


def pick(total, unit, limit):
    best = total
    if total % unit == 0:
        for size in range(unit, min(total, limit) + 1, unit):
            if total % size == 0:
                best = size
    return best


def map_tokens(lam, query_out, query_in, out_tokens, row_tiles, col_tiles):
    rows, cols = lam.shape[1:]
    queries, depth = query_in.shape[:2]
    tokens = sum(part.shape[0] for part in out_tokens)
    height = pick(rows, 128, 256)
    if cols % 128:
        col_part = lax.rem(lax.axis_index("cand"), col_tiles)
        query_in = lax.dynamic_slice_in_dim(query_in, col_part * cols, cols, 2)
    grant = (16 << 20) + 4 * queries * tokens * cols + 4 * height * cols
    resident = pl.BlockSpec(memory_space=pltpu.VMEM)
    return pl.pallas_call(
        functools.partial(map_kernel, row_tiles=row_tiles, col_tiles=col_tiles),
        grid=(rows // height,),
        in_specs=[
            pl.BlockSpec((1, height, cols), lambda i: (0, i, 0)),
            whole(query_out),
            whole(query_in),
            *[resident] * len(out_tokens),
        ],
        out_specs=resident,
        out_shape=jax.ShapeDtypeStruct((queries, tokens, cols), jnp.float32),
        scratch_shapes=[
            pltpu.VMEM((tokens, rows), jnp.bfloat16),
            pltpu.VMEM((min(BEHIND, queries), height, min(PIECE, cols)), jnp.bfloat16),
        ],
        compiler_params=pltpu.CompilerParams(vmem_limit_bytes=grant),
        cost_estimate=pl.CostEstimate(
            flops=2 * queries * rows * cols * 512,
            bytes_accessed=2 * rows * cols,
            transcendentals=rows * cols,
        ),
    )(lam, in_hbm(query_out), in_hbm(query_in), *out_tokens)


def fold_kernel(live_ref, mapped_ref, *refs, by_shift, per_slot):
    queries = mapped_ref.shape[0]
    token_refs = refs[: len(refs) // 2]
    position = lax.axis_index("cand")
    start = 0
    for index, in_ref in enumerate(token_refs):
        rows = in_ref.shape[0]
        inside = in_ref[...].astype(jnp.float32)
        sums = [
            jnp.sum(mapped_ref[q, start : start + rows, :] * inside, axis=1, keepdims=True)
            for q in range(queries)
        ]
        start += rows
        if not by_shift:
            for q in range(queries):
                refs[-1][q, :] = sums[q][:, 0]
            continue
        lane = lax.broadcasted_iota(jnp.int32, (rows, queries), 1)
        table = sum(jnp.where(lane == q, sums[q], 0.0) for q in range(queries))
        sources = len(token_refs)
        live = live_ref[0, lax.rem(position + sources - index, sources)]
        target = refs[sources + index]
        for slot in range(rows // per_slot):
            part = table[slot * per_slot : (slot + 1) * per_slot]
            total = jnp.sum(part, axis=0, keepdims=True)
            target[slot : slot + 1, :] = jnp.where(slot < live, total, 0.0)


def fold_tokens(live_counts, mapped, in_tokens, per_slot, by_shift):
    queries, tokens, cols = mapped.shape
    grant = min((8 << 20) + 12 * queries * tokens * cols, 60 << 20)
    resident = pl.BlockSpec(memory_space=pltpu.VMEM)
    if by_shift:
        shape = (in_tokens[0].shape[0] // per_slot, queries)
        results = [jax.ShapeDtypeStruct(shape, jnp.float32)] * len(in_tokens)
    else:
        results = [jax.ShapeDtypeStruct((queries, tokens), jnp.float32)]
    return pl.pallas_call(
        functools.partial(fold_kernel, by_shift=by_shift, per_slot=per_slot),
        in_specs=[pl.BlockSpec(memory_space=pltpu.SMEM)] + [resident] * (1 + len(in_tokens)),
        out_specs=[resident] * len(results),
        out_shape=results,
        compiler_params=pltpu.CompilerParams(vmem_limit_bytes=grant),
    )(in_hbm(live_counts), mapped, *in_tokens)


def exchange(array):
    return lax.all_to_all(array, "cand", split_axis=0, concat_axis=0, tiled=True)


def shifted(array, shift, devices):
    pairs = [(device, (device + shift) % devices) for device in range(devices)]
    return lax.ppermute(array, "cand", pairs)


def body(cand_out, cand_in, query_out, query_in, eigenvalues, slot_blocks, live_counts):
    tile_count = lax.axis_size("cand")
    row_tiles = min(8, max(2, tile_count // 8))
    col_tiles = tile_count // row_tiles
    tokens = cand_out.shape[1]
    slot_count = slot_blocks.shape[2]
    queries = query_out.shape[0]
    by_shift = tile_count <= MAX_SHIFTS

    packed = pack_tokens(
        cand_out, cand_in, slot_blocks, row_tiles, col_tiles, tile_count, by_shift
    )
    if by_shift:
        out_tokens, in_tokens = [
            [group[0]] + [shifted(group[s], s, tile_count) for s in range(1, tile_count)]
            for group in (packed[:tile_count], packed[tile_count:])
        ]
    else:
        out_tokens, in_tokens = [
            [exchange(group).reshape(-1, group.shape[2])] for group in packed
        ]
    mapped = map_tokens(eigenvalues, query_out, query_in, out_tokens, row_tiles, col_tiles)
    parts = fold_tokens(live_counts, mapped, in_tokens, tokens, by_shift)
    if by_shift:
        total = parts[0]
        for shift in range(1, tile_count):
            total = total + shifted(parts[shift], -shift, tile_count)
        return jnp.transpose(total[None], (2, 0, 1))
    split = jnp.moveaxis(parts[0].reshape(queries, tile_count, -1), 1, 0)
    total = jnp.sum(exchange(split), axis=0)
    scores = total.reshape(queries, slot_count, tokens).sum(axis=2)
    position = lax.axis_index("cand")
    own_live = lax.dynamic_index_in_dim(live_counts[0], position, 0, keepdims=False)
    used = jnp.arange(slot_count, dtype=jnp.int32) < own_live
    return jnp.where(used[None], scores, 0.0)[:, None, :]


def solution(mesh):
    return jax.shard_map(
        body,
        mesh=mesh,
        in_specs=(
            P(("parts", "cand"), None, None),
            P(("parts", "cand"), None, None),
            P(("parts", "query"), None, None),
            P(("parts", "query"), None, None),
            P("cand", None, None),
            P(("parts", "query"), None, None),
            P(("parts", "query"), None),
        ),
        out_specs=P(("parts", "query"), "cand", None),
        check_vma=False,
    )
```

```python
import functools

import jax
import jax.numpy as jnp
from jax import lax
from jax.experimental import pallas as pl
from jax.experimental.pallas import tpu as pltpu
from jax.sharding import PartitionSpec as P

DAMPING = 0.05
PIECE = 512
BEHIND = 2
MAX_SHIFTS = 8
GRANT_PACK = 16 << 20


def pack_kernel(list_ref, out_ref, in_ref, *results, row_tiles, col_tiles, shifts, by_shift):
    position = lax.axis_index("cand")
    slots = list_ref.shape[1]
    tokens = out_ref.shape[1]
    row_width = out_ref.shape[2] // row_tiles
    col_width = in_ref.shape[2] // col_tiles

    def store(source, target, part, width, parts):
        for piece in range(parts):

            @pl.when(part == piece)
            def _():
                for slot in range(slots):
                    block = list_ref[0, slot, position]
                    target[slot * tokens : (slot + 1) * tokens, :] = source[
                        block, :, piece * width : (piece + 1) * width
                    ]

    for shift in range(shifts):
        if by_shift:
            tile = lax.rem(position + shift, shifts)
            targets = results[shift], results[shifts + shift]
        else:
            tile = jnp.int32(shift)
            targets = results[0].at[shift], results[1].at[shift]
        store(out_ref, targets[0], tile // col_tiles, row_width, row_tiles)
        store(in_ref, targets[1], lax.rem(tile, col_tiles), col_width, col_tiles)


def in_hbm(array):
    return pltpu.with_memory_space_constraint(array, pltpu.HBM)


def whole(array):
    return pl.BlockSpec(array.shape, lambda *i: (0,) * len(array.shape))


def pack_tokens(cand_out, cand_in, slot_blocks, row_tiles, col_tiles, shifts, by_shift):
    lists = jnp.swapaxes(slot_blocks, 1, 2)
    rows = slot_blocks.shape[2] * cand_out.shape[1]
    widths = cand_out.shape[2] // row_tiles, cand_in.shape[2] // col_tiles
    if by_shift:
        shapes = [(rows, width) for width in widths for _ in range(shifts)]
    else:
        shapes = [(shifts, rows, width) for width in widths]
    results = [jax.ShapeDtypeStruct(shape, cand_out.dtype) for shape in shapes]
    return pl.pallas_call(
        functools.partial(
            pack_kernel,
            row_tiles=row_tiles,
            col_tiles=col_tiles,
            shifts=shifts,
            by_shift=by_shift,
        ),
        grid=(1,),
        in_specs=[pl.BlockSpec(memory_space=pltpu.SMEM), whole(cand_out), whole(cand_in)],
        out_specs=[pl.BlockSpec(memory_space=pltpu.VMEM)] * len(results),
        out_shape=results,
        compiler_params=pltpu.CompilerParams(vmem_limit_bytes=GRANT_PACK),
    )(in_hbm(lists), in_hbm(cand_out), in_hbm(cand_in))


class Factors:
    def __init__(self, left_ref, right_ref, height, cols, row_tiles, col_tiles):
        position = lax.axis_index("cand")
        self.left_ref, self.right_ref = left_ref, right_ref
        self.height, self.cols = height, cols
        self.row_start = (position // col_tiles) * (left_ref.shape[2] // row_tiles)
        self.split = right_ref.shape[2] != cols
        self.col_start = lax.rem(position, col_tiles) * cols

    def left(self, query, block):
        start = pl.multiple_of(self.row_start + block * self.height, 128)
        rows = self.left_ref[query, :, pl.ds(start, self.height)]
        return rows.astype(jnp.float32).T.astype(jnp.bfloat16)

    def right(self, query, begin, end):
        if not self.split:
            return self.right_ref[query, :, begin:end]
        start = pl.multiple_of(self.col_start + begin, 128)
        return self.right_ref[query, :, pl.ds(start, end - begin)]


def map_kernel(lam_ref, left_ref, right_ref, *refs, row_tiles, col_tiles):
    token_refs, (acc_ref, token_buf, held) = refs[:-3], refs[-3:]
    queries, height, cols = left_ref.shape[0], lam_ref.shape[1], lam_ref.shape[2]
    step = pl.program_id(0)

    @pl.when(step == 0)
    def _():
        held[...] = jnp.zeros_like(held)
        start = 0
        for ref in token_refs:
            token_buf[start : start + ref.shape[0], :] = ref[...]
            start += ref.shape[0]

    factors = Factors(left_ref, right_ref, height, cols, row_tiles, col_tiles)
    lefts = [factors.left(q, step) for q in range(queries)]
    behind = held.shape[0]
    pieces = [(begin, min(begin + PIECE, cols)) for begin in range(0, cols, PIECE)]
    begin, end = pieces[-1]

    def token_rows(block):
        return token_buf[:, pl.ds(pl.multiple_of(block * height, 128), height)]

    rows, rows_before = token_rows(step), token_rows(jnp.maximum(step - 1, 0))
    carried = range(queries - behind, queries)
    waiting = [
        (q, begin, end, rows_before, held[slot, :, : end - begin]) for slot, q in enumerate(carried)
    ]

    touched = set()

    def contract():
        q, begin, end, mine, precond = waiting.pop(0)
        fresh = (q, begin) not in touched
        touched.add((q, begin))
        before = jnp.where(step > 0, acc_ref[q, :, begin:end], 0.0) if fresh else acc_ref[q, :, begin:end]
        acc_ref[q, :, begin:end] = before + jnp.dot(
            mine, precond, preferred_element_type=jnp.float32
        )

    for begin, end in pieces:
        inverse = 1.0 / (lam_ref[0, :, begin:end].astype(jnp.float32) + DAMPING)
        for q in range(queries):
            outer = jnp.dot(
                lefts[q], factors.right(q, begin, end), preferred_element_type=jnp.float32
            )
            contract()
            waiting.append((q, begin, end, rows, (outer * inverse).astype(jnp.bfloat16)))
    for slot, item in enumerate(waiting):
        assert (item[0], item[1]) in touched
        held[slot, :, : end - begin] = item[-1]

    @pl.when(step == pl.num_programs(0) - 1)
    def _():
        for slot, q in enumerate(carried):
            acc_ref[q, :, begin:end] += jnp.dot(
                rows, held[slot, :, : end - begin], preferred_element_type=jnp.float32
            )


def pick(total, unit, limit):
    best = total
    if total % unit == 0:
        for size in range(unit, min(total, limit) + 1, unit):
            if total % size == 0:
                best = size
    return best


def map_tokens(lam, query_out, query_in, out_tokens, row_tiles, col_tiles):
    rows, cols = lam.shape[1:]
    queries, depth = query_in.shape[:2]
    tokens = sum(part.shape[0] for part in out_tokens)
    height = pick(rows, 128, 256)
    if cols % 128:
        col_part = lax.rem(lax.axis_index("cand"), col_tiles)
        query_in = lax.dynamic_slice_in_dim(query_in, col_part * cols, cols, 2)
    grant = (16 << 20) + 4 * queries * tokens * cols + 4 * height * cols
    resident = pl.BlockSpec(memory_space=pltpu.VMEM)
    return pl.pallas_call(
        functools.partial(map_kernel, row_tiles=row_tiles, col_tiles=col_tiles),
        grid=(rows // height,),
        in_specs=[
            pl.BlockSpec((1, height, cols), lambda i: (0, i, 0)),
            whole(query_out),
            whole(query_in),
            *[resident] * len(out_tokens),
        ],
        out_specs=resident,
        out_shape=jax.ShapeDtypeStruct((queries, tokens, cols), jnp.float32),
        scratch_shapes=[
            pltpu.VMEM((tokens, rows), jnp.bfloat16),
            pltpu.VMEM((min(BEHIND, queries), height, min(PIECE, cols)), jnp.bfloat16),
        ],
        compiler_params=pltpu.CompilerParams(vmem_limit_bytes=grant),
        cost_estimate=pl.CostEstimate(
            flops=2 * queries * rows * cols * 512,
            bytes_accessed=2 * rows * cols,
            transcendentals=rows * cols,
        ),
    )(lam, in_hbm(query_out), in_hbm(query_in), *out_tokens)


def fold_kernel(live_ref, mapped_ref, *refs, by_shift, per_slot):
    queries = mapped_ref.shape[0]
    token_refs = refs[: len(refs) // 2]
    position = lax.axis_index("cand")
    start = 0
    for index, in_ref in enumerate(token_refs):
        rows = in_ref.shape[0]
        inside = in_ref[...].astype(jnp.float32)
        sums = [
            jnp.sum(mapped_ref[q, start : start + rows, :] * inside, axis=1, keepdims=True)
            for q in range(queries)
        ]
        start += rows
        if not by_shift:
            for q in range(queries):
                refs[-1][q, :] = sums[q][:, 0]
            continue
        lane = lax.broadcasted_iota(jnp.int32, (rows, queries), 1)
        table = sum(jnp.where(lane == q, sums[q], 0.0) for q in range(queries))
        sources = len(token_refs)
        live = live_ref[0, lax.rem(position + sources - index, sources)]
        target = refs[sources + index]
        for slot in range(rows // per_slot):
            part = table[slot * per_slot : (slot + 1) * per_slot]
            total = jnp.sum(part, axis=0, keepdims=True)
            target[slot : slot + 1, :] = jnp.where(slot < live, total, 0.0)


def fold_tokens(live_counts, mapped, in_tokens, per_slot, by_shift):
    queries, tokens, cols = mapped.shape
    grant = min((8 << 20) + 12 * queries * tokens * cols, 60 << 20)
    resident = pl.BlockSpec(memory_space=pltpu.VMEM)
    if by_shift:
        shape = (in_tokens[0].shape[0] // per_slot, queries)
        results = [jax.ShapeDtypeStruct(shape, jnp.float32)] * len(in_tokens)
    else:
        results = [jax.ShapeDtypeStruct((queries, tokens), jnp.float32)]
    return pl.pallas_call(
        functools.partial(fold_kernel, by_shift=by_shift, per_slot=per_slot),
        in_specs=[pl.BlockSpec(memory_space=pltpu.SMEM)] + [resident] * (1 + len(in_tokens)),
        out_specs=[resident] * len(results),
        out_shape=results,
        compiler_params=pltpu.CompilerParams(vmem_limit_bytes=grant),
    )(in_hbm(live_counts), mapped, *in_tokens)


def exchange(array):
    return lax.all_to_all(array, "cand", split_axis=0, concat_axis=0, tiled=True)


def shifted(array, shift, devices):
    pairs = [(device, (device + shift) % devices) for device in range(devices)]
    return lax.ppermute(array, "cand", pairs)


def body(cand_out, cand_in, query_out, query_in, eigenvalues, slot_blocks, live_counts):
    tile_count = lax.axis_size("cand")
    row_tiles = min(8, max(2, tile_count // 8))
    col_tiles = tile_count // row_tiles
    tokens = cand_out.shape[1]
    slot_count = slot_blocks.shape[2]
    queries = query_out.shape[0]
    by_shift = tile_count <= MAX_SHIFTS

    packed = pack_tokens(
        cand_out, cand_in, slot_blocks, row_tiles, col_tiles, tile_count, by_shift
    )
    if by_shift:
        out_tokens, in_tokens = [
            [group[0]] + [shifted(group[s], s, tile_count) for s in range(1, tile_count)]
            for group in (packed[:tile_count], packed[tile_count:])
        ]
    else:
        out_tokens, in_tokens = [
            [exchange(group).reshape(-1, group.shape[2])] for group in packed
        ]
    mapped = map_tokens(eigenvalues, query_out, query_in, out_tokens, row_tiles, col_tiles)
    parts = fold_tokens(live_counts, mapped, in_tokens, tokens, by_shift)
    if by_shift:
        total = parts[0]
        for shift in range(1, tile_count):
            total = total + shifted(parts[shift], -shift, tile_count)
        return jnp.transpose(total[None], (2, 0, 1))
    split = jnp.moveaxis(parts[0].reshape(queries, tile_count, -1), 1, 0)
    total = jnp.sum(exchange(split), axis=0)
    scores = total.reshape(queries, slot_count, tokens).sum(axis=2)
    position = lax.axis_index("cand")
    own_live = lax.dynamic_index_in_dim(live_counts[0], position, 0, keepdims=False)
    used = jnp.arange(slot_count, dtype=jnp.int32) < own_live
    return jnp.where(used[None], scores, 0.0)[:, None, :]


def solution(mesh):
    return jax.shard_map(
        body,
        mesh=mesh,
        in_specs=(
            P(("parts", "cand"), None, None),
            P(("parts", "cand"), None, None),
            P(("parts", "query"), None, None),
            P(("parts", "query"), None, None),
            P("cand", None, None),
            P(("parts", "query"), None, None),
            P(("parts", "query"), None),
        ),
        out_specs=P(("parts", "query"), "cand", None),
        check_vma=False,
    )
```
